512 devices in a mesh: layer: 8 (over x, core), rows: 64 (over z, y).
Axes of the slice: x: 4, y: 4, z: 16, core: 2. Of those that a mesh axis runs over, the one named last changes fastest.
Arguments:
- down_sources: bfloat16 [8, 32, 16384], P('layer', None, 'rows'), may hold values from -6 to 6
- up_sources: bfloat16 [8, 32, 16384], P('layer', None, 'rows'), may hold values from -6 to 6
- down_tiles: bfloat16 [8, 1024, 128, 128], P('layer', 'rows'), may hold values from -0.1875 to 0.1875
- up_tiles: bfloat16 [8, 1024, 128, 128], P('layer', 'rows'), may hold values from -0.1875 to 0.1875
- tile_rows: int32 [8, 1024], P('layer', 'rows'), may hold values from 0 to 127, as said below
- tile_cols: int32 [8, 1024], P('layer', 'rows'), may hold values from 0 to 127, as said below
- shot_order: int32 [32], replicated, may hold values from 0 to 31, each once
Outputs:
- traces: bfloat16 [8, 32, 16384], P('layer', None, 'rows')
The draws below stay inside these ranges and needn't reach their ends.
Inputs may be any that keep to these rules, and one draw needn't show every extreme that they name: `tile_rows`: in every layer, tile t lies in the tile rows of index t // 16 of the rows axis: 2 * (t // 16) to 2 * (t // 16) + 1. `tile_cols`: every tile's column differs from its row by at most 2. `shot_order`: A permutation of the shots.
All inputs are finite; a program needn't handle non-finite values.
Results may differ from the reference program's by a relative error of at most 0.011.
Values may be sent and summed in bfloat16 or wider, within the bound.
A program may use at most 64 MiB of HBM per device.

```python
import jax
import jax.numpy as jnp
from jax import lax

M = 16384
TILE = 128
TILES = 1024
SHOTS = 32
TROWS = 128
TR_DEV = 2
TILES_DEV = 16
LAYERS = 8


def tile_layout(key):
    owner = jnp.arange(TILES, dtype=jnp.int32) // TILES_DEV
    within = jax.random.randint(jax.random.fold_in(key, 11), (LAYERS, TILES), 0, TR_DEV, dtype=jnp.int32)
    rows = owner[None, :] * TR_DEV + within
    offset = jax.random.randint(jax.random.fold_in(key, 12), (LAYERS, TILES), -TR_DEV, TR_DEV + 1, dtype=jnp.int32)
    cols = jnp.clip(rows + offset, 0, TROWS - 1)
    return (rows, cols)


def draw_tile_rows(key, part):
    return tile_layout(key)[0]


def draw_tile_cols(key, part):
    return tile_layout(key)[1]


def shard_levels(stream_key, shape, shards, smallest, high):
    def one(axis_at, parts):
        draws = jax.random.uniform(jax.random.fold_in(jax.random.fold_in(stream_key, 6), axis_at), (parts,), jnp.float32, smallest / len(shards), high / len(shards))
        return jnp.repeat(jnp.exp(draws), shape[axis_at] // parts).reshape((-1,) + (1,) * (len(shape) - axis_at - 1))

    level = one(*shards[0])
    for cut in shards[1:]:
        level = level * one(*cut)
    return level


def scatter_about(own_key, extent, width, reach, shards=(), kind=jnp.bfloat16):
    entries = width * jax.random.normal(own_key, extent, jnp.float32)
    if shards:
        entries = entries * shard_levels(own_key, extent, shards, -0.22, 0.18)
    return jnp.clip(entries, -reach, reach).astype(kind)


def setup_inputs(seed: int = 0) -> dict:
    seeds = jax.random.split(jax.random.key(seed), 8)
    down_sources = scatter_about(seeds[0], (LAYERS, SHOTS, M), 1.0, 6.0, ((0, 8), (2, 64)))
    up_sources = scatter_about(seeds[1], (LAYERS, SHOTS, M), 1.0, 6.0, ((0, 8), (2, 64)))
    down_tiles = scatter_about(seeds[2], (LAYERS, TILES, TILE, TILE), (TILE * TILES // TROWS) ** -0.5, 0.1875, ((0, 8), (1, 64)))
    up_tiles = scatter_about(seeds[3], (LAYERS, TILES, TILE, TILE), (TILE * TILES // TROWS) ** -0.5, 0.1875, ((0, 8), (1, 64)))
    tile_rows = draw_tile_rows(jax.random.fold_in(seeds[7], 71), 0)
    tile_cols = draw_tile_cols(jax.random.fold_in(seeds[7], 71), 0)
    shot_order = jax.random.permutation(seeds[6], SHOTS).astype(jnp.int32)
    return {"down_sources": down_sources, "up_sources": up_sources, "down_tiles": down_tiles, "up_tiles": up_tiles, "tile_rows": tile_rows, "tile_cols": tile_cols, "shot_order": shot_order}


def apply_layer(tiles, rows, cols, trace):
    blocks = trace.reshape(SHOTS, TROWS, TILE)
    picked = jnp.take(blocks, cols.astype(jnp.int32), axis=1).astype(jnp.float32)
    product = jnp.einsum('tij,stj->sti', tiles.astype(jnp.float32), picked, precision=lax.Precision.HIGHEST)
    onehot = (rows[:, None] == jnp.arange(TROWS, dtype=jnp.int32)[None, :]).astype(jnp.float32)
    summed = jnp.einsum('sti,tr->sri', product, onehot, precision=lax.Precision.HIGHEST)
    return summed.reshape(SHOTS, M)


def reference(down_sources, up_sources, down_tiles, up_tiles, tile_rows, tile_cols, shot_order):
    order = shot_order.astype(jnp.int32)
    forward = jnp.take(down_sources, order, axis=1)
    backward = jnp.take(up_sources, order, axis=1)
    downs = [forward[0]]
    for layer in range(1, LAYERS):
        term = apply_layer(down_tiles[layer], tile_rows[layer], tile_cols[layer], downs[-1])
        downs.append((forward[layer].astype(jnp.float32) + term).astype(jnp.bfloat16))
    ups = [backward[LAYERS - 1]]
    for layer in range(LAYERS - 2, -1, -1):
        term = apply_layer(up_tiles[layer], tile_rows[layer], tile_cols[layer], ups[-1])
        ups.append((backward[layer].astype(jnp.float32) + term).astype(jnp.bfloat16))
    ups = ups[::-1]
    result = [(downs[k].astype(jnp.float32) + ups[k].astype(jnp.float32)).astype(jnp.bfloat16) for k in range(LAYERS)]
    return jnp.stack(result, axis=0)
```

```python
import functools

import jax
import jax.numpy as jnp
from jax import lax
from jax.experimental import pallas as pl
from jax.experimental.pallas import tpu as pltpu
from jax.sharding import PartitionSpec as P

TILE = 128
MESH = pl.DeviceIdType.MESH
F32 = jnp.float32
BF16 = jnp.bfloat16


def kernel(
    rows_ref,
    cols_ref,
    order_ref,
    down_src,
    up_src,
    down_tiles,
    up_tiles,
    out_ref,
    src,
    own,
    tiles,
    band,
    recv,
    trace,
    src_sem,
    tile_sem,
    send_sem,
    recv_sem,
):
    layers, devices = lax.axis_size("layer"), lax.axis_size("rows")
    layer, k = lax.axis_index("layer"), lax.axis_index("rows")
    shots, width = own.shape[1], own.shape[2]
    local = width // TILE
    count = tiles.shape[1]

    src_copies = [
        pltpu.make_async_copy(ref.at[0], src.at[d], src_sem.at[d])
        for d, ref in enumerate((down_src, up_src))
    ]
    tile_copies = [
        pltpu.make_async_copy(ref.at[0], tiles.at[d], tile_sem.at[d])
        for d, ref in enumerate((down_tiles, up_tiles))
    ]
    for copy in src_copies + tile_copies:
        copy.start()

    barrier = pltpu.get_barrier_semaphore()

    def inside(dl, dk):
        return (
            (layer + dl >= 0) & (layer + dl < layers) & (k + dk >= 0) & (k + dk < devices)
        )

    for dl in (-1, 1):
        for dk in (-1, 1, 0):

            @pl.when(inside(dl, dk))
            def _():
                pl.semaphore_signal(
                    barrier, inc=1, device_id=(layer + dl, k + dk), device_id_type=MESH
                )

    @pl.when(k == 0)
    def _():
        for d in range(2):
            recv[d, 0] = jnp.zeros_like(recv[d, 0])

    @pl.when(k == devices - 1)
    def _():
        for d in range(2):
            recv[d, 2] = jnp.zeros_like(recv[d, 2])

    slot_of = lax.broadcasted_iota(jnp.int32, (shots, shots), 0)
    shot_of = lax.broadcasted_iota(jnp.int32, (shots, shots), 1)
    wanted = jnp.zeros((shots, shots), jnp.int32)
    for j in range(shots):
        wanted = jnp.where(slot_of == j, order_ref[j], wanted)
    pick = (shot_of == wanted).astype(F32).astype(BF16)
    for d in range(2):
        src_copies[d].wait()
        own[d] = jnp.dot(pick, src[d], preferred_element_type=F32).astype(BF16)

    def out_copy(d, dk):
        dl = 1 - 2 * d
        return pltpu.make_async_remote_copy(
            src_ref=trace.at[d],
            dst_ref=recv.at[d, 1 - dk],
            send_sem=send_sem.at[d, 1 - dk],
            recv_sem=recv_sem.at[d, 1 - dk],
            device_id=(layer + dl, k + dk),
            device_id_type=MESH,
        )

    def each_target(d, act):
        dl = 1 - 2 * d
        for dk in (-1, 1, 0):

            @pl.when(inside(dl, dk))
            def _():
                act(out_copy(d, dk))

    partners = ((layer > 0).astype(jnp.int32) + (layer < layers - 1).astype(jnp.int32)) * (
        1 + (k > 0).astype(jnp.int32) + (k < devices - 1).astype(jnp.int32)
    )
    pl.semaphore_wait(barrier, partners)

    for d, head in ((0, 0), (1, layers - 1)):

        @pl.when(layer == head)
        def _():
            trace[d] = own[d]
            each_target(d, lambda copy: copy.start())

    span = 3 * local
    place = []
    for t in range(count):
        row = rows_ref[0, t] - k * local
        col = cols_ref[0, t] - (k - 1) * local
        place.append(row * span + col)
    for d in range(2):
        tile_copies[d].wait()

    def build(step, carry):
        d, part = step // 8, step % 8
        lines = pl.ds(pl.multiple_of(part * 16, 16), 16)
        pieces = [tiles[d, t, lines, :].astype(F32) for t in range(count)]
        for r in range(local):
            for c in range(span):
                at = (d, c // local, pl.ds(pl.multiple_of(part * 16 + r * TILE, 16), 16))
                lanes = pl.ds((c % local) * TILE, TILE)
                if abs(c - local - r) > 2:
                    band[(*at, lanes)] = jnp.zeros((16, TILE), BF16)
                    continue
                total = jnp.zeros((16, TILE), F32)
                for t in range(count):
                    total = total + jnp.where(place[t] == r * span + c, pieces[t], 0.0)
                band[(*at, lanes)] = total.astype(BF16)
        return carry

    lax.fori_loop(0, 16, build, 0)

    for event in range(2):
        d = (layer // (layers // 2) + event) % 2
        head = d * (layers - 1)

        @pl.when(layer != head)
        def _():
            total = own[d].astype(F32)
            for b in (1, 0, 2):

                @pl.when((k - 1 + b >= 0) & (k - 1 + b < devices))
                def _():
                    pltpu.make_async_remote_copy(
                        src_ref=recv.at[d, b],
                        dst_ref=recv.at[d, b],
                        send_sem=send_sem.at[d, b],
                        recv_sem=recv_sem.at[d, b],
                        device_id=(layer, k),
                        device_id_type=MESH,
                    ).wait_recv()

                total = total + lax.dot_general(
                    recv[d, b], band[d, b], (((1,), (1,)), ((), ())), preferred_element_type=F32
                )
            trace[d] = total.astype(BF16)
            each_target(d, lambda copy: copy.start())

    out_ref[0] = (trace[0].astype(F32) + trace[1].astype(F32)).astype(BF16)
    for d in range(2):
        each_target(d, lambda copy: copy.wait_send())


def shards(down_sources, up_sources, down_tiles, up_tiles, tile_rows, tile_cols, shot_order):
    shots, width = down_sources.shape[1:]
    count = down_tiles.shape[1]
    anywhere = pl.BlockSpec(memory_space=pl.ANY)
    scalars = pl.BlockSpec(memory_space=pltpu.SMEM)
    return pl.pallas_call(
        kernel,
        name="sweeps",
        out_shape=jax.ShapeDtypeStruct(down_sources.shape, BF16),
        in_specs=[scalars] * 3 + [anywhere] * 4,
        out_specs=pl.BlockSpec(memory_space=pltpu.VMEM),
        scratch_shapes=[
            pltpu.VMEM((2, shots, width), BF16),
            pltpu.VMEM((2, shots, width), BF16),
            pltpu.VMEM((2, count, TILE, TILE), BF16),
            pltpu.VMEM((2, 3, width, width), BF16),
            pltpu.VMEM((2, 3, shots, width), BF16),
            pltpu.VMEM((2, shots, width), BF16),
            pltpu.SemaphoreType.DMA((2,)),
            pltpu.SemaphoreType.DMA((2,)),
            pltpu.SemaphoreType.DMA((2, 3)),
            pltpu.SemaphoreType.DMA((2, 3)),
        ],
        compiler_params=pltpu.CompilerParams(collective_id=0, has_side_effects=True),
    )(tile_rows, tile_cols, shot_order, down_sources, up_sources, down_tiles, up_tiles)


def solution(mesh):
    return jax.shard_map(
        shards,
        mesh=mesh,
        in_specs=(
            P("layer", None, "rows"),
            P("layer", None, "rows"),
            P("layer", "rows", None, None),
            P("layer", "rows", None, None),
            P("layer", "rows"),
            P("layer", "rows"),
            P(),
        ),
        out_specs=P("layer", None, "rows"),
        check_vma=False,
    )
```

```python
import jax
import jax.numpy as jnp
from jax import lax
from jax.experimental import pallas as pl
from jax.experimental.pallas import tpu as pltpu
from jax.sharding import PartitionSpec as P

TILE = 128
MESH = pl.DeviceIdType.MESH
F32 = jnp.float32
BF16 = jnp.bfloat16
LEFT, HOME, RIGHT, SECOND, OTHER = range(5)
PART = 16


def band_rows(c, r):
    return 0 if c == 0 else TILE + 2 * TILE * (c - 1) + (r * TILE if c < 5 else 0)


def band_block(bands, slot, b):
    def tile(c, r):
        return bands[slot, pl.ds(band_rows(c, r), TILE), :]

    def line(r):
        pieces = [
            tile(c, r) if abs(c - 2 - r) <= 2 else jnp.zeros((TILE, TILE), BF16)
            for c in (2 * b, 2 * b + 1)
        ]
        return jnp.concatenate(pieces, axis=1)

    return jnp.concatenate([line(0), line(1)], axis=0)


def times(block, bands, slot, b):
    return lax.dot_general(
        block, band_block(bands, slot, b), (((1,), (1,)), ((), ())), preferred_element_type=F32
    )


def kernel(
    rows_hbm,
    cols_hbm,
    order_hbm,
    down_src,
    up_src,
    down_tiles,
    up_tiles,
    out_ref,
    rows_ref,
    cols_ref,
    order_ref,
    src,
    tiles,
    bands,
    terms,
    first,
    second,
    arrived,
    handed,
    scalar_sem,
    src_sem,
    tile_sem,
    band_send,
    band_recv,
    term_send,
    term_recv,
    source_send,
    source_recv,
    trace_send,
    trace_recv,
    hand_send,
    hand_recv,
    go,
):
    devices = lax.axis_size("rows")
    layer, k = lax.axis_index("layer"), lax.axis_index("rows")
    shots, width = src.shape[1], src.shape[2]
    local = width // TILE
    count = tiles.shape[1]

    x, core = layer // 2, layer % 2
    partner = 1 - core
    outer = (x == 0) | (x == 3)
    mine = jnp.where(outer, partner, core)
    X = jnp.where(mine == 0, x, 3 - x)
    ahead = 1 - 2 * mine
    mid = jnp.logical_not(outer)

    scalar_copies = [
        pltpu.make_async_copy(a, b, scalar_sem.at[i])
        for i, (a, b) in enumerate(
            ((rows_hbm, rows_ref), (cols_hbm, cols_ref), (order_hbm, order_ref))
        )
    ]
    src_copies = [
        pltpu.make_async_copy(ref.at[0], src.at[d], src_sem.at[d])
        for d, ref in enumerate((down_src, up_src))
    ]
    tile_copies = [
        pltpu.make_async_copy(ref.at[0], tiles.at[d], tile_sem.at[d])
        for d, ref in enumerate((down_tiles, up_tiles))
    ]
    for copy in scalar_copies + src_copies + tile_copies:
        copy.start()

    def exists(s):
        return (k + s >= 0) & (k + s < devices)

    def present(s):
        return exists(s).astype(jnp.int32)

    barrier = pltpu.get_barrier_semaphore()

    def greet(condition, x_to, core_to, s):
        @pl.when(condition & exists(s))
        def _():
            pl.semaphore_signal(
                barrier, inc=1, device_id=(x_to * 2 + core_to, k + s), device_id_type=MESH
            )

    for s in (-1, 1, 0):
        greet(True, x, partner if s == 0 else jnp.where(outer, partner, core), s)
    for s in (-2, 2, -1, 1, 0):
        greet(X >= 1, x - ahead, jnp.where(X == 1, 1 - mine, mine), s)

    for s in (-2, -1, 1, 2):

        @pl.when(jnp.logical_not(exists(s)))
        def _():
            arrived[2 + s] = jnp.zeros_like(arrived[2 + s])

    for s in (-1, 1):

        @pl.when(jnp.logical_not(exists(s)))
        def _():
            first[1 + s] = jnp.zeros_like(first[1 + s])
            terms[1 + s] = jnp.zeros_like(terms[1 + s])
            bands[1 + s] = jnp.zeros_like(bands[1 + s])

    for copy in scalar_copies:
        copy.wait()
    slot_of = lax.broadcasted_iota(jnp.int32, (shots, shots), 0)
    shot_of = lax.broadcasted_iota(jnp.int32, (shots, shots), 1)
    wanted = jnp.zeros((shots, shots), jnp.int32)
    for j in range(shots):
        wanted = jnp.where(slot_of == j, order_ref[j], wanted)
    pick = (shot_of == wanted).astype(F32).astype(BF16)
    for copy in src_copies:
        copy.wait()
    own = jnp.where(mid, HOME, SECOND)
    for sweep, slot in ((mine, own), (1 - mine, OTHER)):
        terms[slot] = jnp.dot(pick, src[sweep], preferred_element_type=F32).astype(BF16)

    place = []
    for t in range(count):
        row = rows_ref[t] - k * local
        col = cols_ref[t] - (k - 1) * local
        place.append(row * 3 * local + col)

    steps = TILE // PART

    def build(step, carry):
        other, part = step // steps, step % steps
        sweep = jnp.where(other == 0, mine, 1 - mine)
        slot = jnp.where(other == 0, own, OTHER)
        lines = pl.ds(pl.multiple_of(part * PART, PART), PART)
        pieces = [tiles[sweep, t, lines, :].astype(F32) for t in range(count)]
        for r in range(local):
            for c in range(r, r + 5):
                total = jnp.zeros((PART, TILE), F32)
                for t in range(count):
                    total = total + jnp.where(place[t] == r * 3 * local + c, pieces[t], 0.0)
                at = pl.ds(pl.multiple_of(band_rows(c, r) + part * PART, PART), PART)
                bands[slot, at, :] = total.astype(BF16)
        return carry

    def send(source, target, send_sem, recv_sem, x_to, core_to, s):
        return pltpu.make_async_remote_copy(
            src_ref=source,
            dst_ref=target,
            send_sem=send_sem,
            recv_sem=recv_sem,
            device_id=(x_to * 2 + core_to, k + s),
            device_id_type=MESH,
        )

    def await_recv(buffer, sem):
        pltpu.make_async_remote_copy(
            src_ref=buffer,
            dst_ref=buffer,
            send_sem=hand_send,
            recv_sem=sem,
            device_id=(layer, k),
            device_id_type=MESH,
        ).wait_recv()

    def when_all(condition, copies, act):
        for s, copy in copies:

            @pl.when(condition & exists(s))
            def _():
                act(copy(s))

    start = lambda copy: copy.start()
    wait_send = lambda copy: copy.wait_send()

    def near_term(s):
        return send(terms.at[HOME], terms.at[1 - s], term_send.at[1 + s], term_recv.at[1 - s], x, core, s)

    def near_band(s):
        return send(bands.at[HOME], bands.at[1 - s], band_send.at[1 + s], band_recv.at[1 - s], x, core, s)

    near = [(s, f) for f in (near_term, near_band) for s in (-1, 1)]

    def cross_slot(s):
        return jnp.where(mid, SECOND, 1 - s)

    def cross_term(s):
        to = cross_slot(s)
        return send(terms.at[OTHER], terms.at[to], term_send.at[4 + s], term_recv.at[to], x, partner, s)

    def cross_band(s):
        to = cross_slot(s)
        return send(bands.at[OTHER], bands.at[to], band_send.at[4 + s], band_recv.at[to], x, partner, s)

    cross_mid = [(0, cross_term), (0, cross_band)]
    cross_outer = [(s, f) for f in (cross_term, cross_band) for s in (-1, 1, 0)]

    def source(s):
        return send(
            terms.at[OTHER], first.at[1 - s], source_send.at[1 + s], source_recv.at[1 - s], x, partner, s
        )

    sources = [(s, source) for s in (-1, 1, 0)]

    def forward(s):
        core_to = jnp.where(X == 2, 1 - mine, mine)
        return send(
            second, arrived.at[2 - s], trace_send.at[2 + s], trace_recv.at[2 - s], x + ahead, core_to, s
        )

    forwards = [(s, forward) for s in (-2, 2, -1, 1, 0)]

    def hand(buffer):
        return send(buffer, handed, hand_send, hand_recv, x, partner, 0)

    @pl.when(X < 3)
    def _():
        for copy in tile_copies:
            copy.wait()
        lax.fori_loop(0, 2 * steps, build, 0)

    beside = present(-1) + present(0) + present(1)
    pl.semaphore_wait(
        barrier, beside + jnp.where(X < 3, beside + present(-2) + present(2), 0)
    )

    when_all(X == 3, sources, start)
    when_all(X == 1, near, start)
    when_all(mid, cross_mid, start)

    @pl.when(X == 3)
    def _():
        for copy in tile_copies:
            copy.wait()
        lax.fori_loop(0, steps, build, 0)

    when_all(X == 1, near, wait_send)

    @pl.when(X == 1)
    def _():
        pl.semaphore_signal(go, inc=1, device_id=(x * 2 + partner, k), device_id_type=MESH)

    @pl.when(X == 2)
    def _():
        pl.semaphore_wait(go, 1)

    when_all(X == 2, near, start)

    @pl.when(X == 0)
    def _():
        total = terms[SECOND].astype(F32)
        for b in (1, 0, 2):

            @pl.when(exists(b - 1))
            def _():
                await_recv(first.at[b], source_recv.at[b])

            total = total + times(first[b], bands, SECOND, b)
        second[...] = total.astype(BF16)

    when_all(X == 0, forwards, start)
    when_all(X == 0, cross_outer, start)

    @pl.when(X >= 1)
    def _():
        for slot in (HOME, LEFT, RIGHT, SECOND):
            from_far = mid if slot == SECOND else (X == 3) if slot == HOME else exists(slot - 1)

            @pl.when(from_far)
            def _():
                await_recv(terms.at[slot], term_recv.at[slot])
                await_recv(bands.at[slot], band_recv.at[slot])

        sums = [terms[t].astype(F32) for t in range(3)]
        total = terms[SECOND].astype(F32)
        for block, done in ((2, ()), (1, ()), (3, (1,)), (0, (0,)), (4, (2,))):

            @pl.when(exists(block - 2))
            def _():
                await_recv(arrived.at[block], trace_recv.at[block])

            for t in range(3):
                b = block - t
                if 0 <= b < 3:
                    sums[t] = sums[t] + times(arrived[block], bands, t, b)
            for t in done:
                value = sums[t].astype(BF16)
                first[t] = value
                if t == 1:

                    @pl.when(X == 3)
                    def _():
                        hand(first.at[1]).start()

                total = total + times(value, bands, SECOND, t)
        second[...] = total.astype(BF16)

    when_all(mid, forwards, start)

    @pl.when(mid)
    def _():
        hand(second).start()

    @pl.when(X == 3)
    def _():
        out_ref[0] = (second[...].astype(F32) + terms[OTHER].astype(F32)).astype(BF16)

    @pl.when(X < 3)
    def _():
        await_recv(handed, hand_recv)

    @pl.when(mid)
    def _():
        out_ref[0] = (first[1].astype(F32) + handed[...].astype(F32)).astype(BF16)

    @pl.when(X == 0)
    def _():
        out_ref[0] = (second[...].astype(F32) + handed[...].astype(F32)).astype(BF16)

    when_all(X == 3, sources, wait_send)
    when_all(X == 2, near, wait_send)
    when_all(mid, cross_mid, wait_send)
    when_all(X == 0, cross_outer, wait_send)
    when_all(X < 3, forwards, wait_send)

    @pl.when(X >= 1)
    def _():
        hand(second).wait_send()


def shards(down_sources, up_sources, down_tiles, up_tiles, tile_rows, tile_cols, shot_order):
    shots, width = down_sources.shape[1:]
    count = down_tiles.shape[1]
    anywhere = pl.BlockSpec(memory_space=pl.ANY)
    dma = pltpu.SemaphoreType.DMA
    return pl.pallas_call(
        kernel,
        name="sweeps",
        out_shape=jax.ShapeDtypeStruct(down_sources.shape, BF16),
        in_specs=[anywhere] * 7,
        out_specs=pl.BlockSpec(memory_space=pltpu.VMEM),
        scratch_shapes=[
            pltpu.SMEM((count,), jnp.int32),
            pltpu.SMEM((count,), jnp.int32),
            pltpu.SMEM(shot_order.shape, jnp.int32),
            pltpu.VMEM((2, shots, width), BF16),
            pltpu.VMEM((2, count, TILE, TILE), BF16),
            pltpu.VMEM((5, 10 * TILE, TILE), BF16),
            pltpu.VMEM((5, shots, width), BF16),
            pltpu.VMEM((3, shots, width), BF16),
            pltpu.VMEM((shots, width), BF16),
            pltpu.VMEM((5, shots, width), BF16),
            pltpu.VMEM((shots, width), BF16),
            dma((3,)),
            dma((2,)),
            dma((2,)),
            dma((6,)),
            dma((4,)),
            dma((6,)),
            dma((4,)),
            dma((3,)),
            dma((3,)),
            dma((5,)),
            dma((5,)),
            dma,
            dma,
            pltpu.SemaphoreType.REGULAR,
        ],
        compiler_params=pltpu.CompilerParams(collective_id=0, has_side_effects=True),
    )(tile_rows[0], tile_cols[0], shot_order, down_sources, up_sources, down_tiles, up_tiles)


def solution(mesh):
    return jax.shard_map(
        shards,
        mesh=mesh,
        in_specs=(
            P("layer", None, "rows"),
            P("layer", None, "rows"),
            P("layer", "rows", None, None),
            P("layer", "rows", None, None),
            P("layer", "rows"),
            P("layer", "rows"),
            P(),
        ),
        out_specs=P("layer", None, "rows"),
        check_vma=False,
    )
```

```python
import jax
import jax.numpy as jnp
from jax import lax
from jax.experimental import pallas as pl
from jax.experimental.pallas import tpu as pltpu
from jax.sharding import PartitionSpec as P

TILE = 128
MESH = pl.DeviceIdType.MESH
F32 = jnp.float32
BF16 = jnp.bfloat16
LEFT, HOME, RIGHT, SECOND = range(4)
SLOTS = 4
OUTGOING = 2 * SLOTS
PART = 16


def band_rows(c, r):
    return 0 if c == 0 else TILE + 2 * TILE * (c - 1) + (r * TILE if c < 5 else 0)


def band_block(bands, slot, b):
    def tile(c, r):
        return bands[slot, pl.ds(band_rows(c, r), TILE), :]

    def line(r):
        pieces = [
            tile(c, r) if abs(c - 2 - r) <= 2 else jnp.zeros((TILE, TILE), BF16)
            for c in (2 * b, 2 * b + 1)
        ]
        return jnp.concatenate(pieces, axis=1)

    return jnp.concatenate([line(0), line(1)], axis=0)


def times(block, bands, slot, b):
    return lax.dot_general(
        block, band_block(bands, slot, b), (((1,), (1,)), ((), ())), preferred_element_type=F32
    )


def kernel(
    rows_hbm,
    cols_hbm,
    order_hbm,
    down_src,
    up_src,
    down_tiles,
    up_tiles,
    out_ref,
    rows_ref,
    cols_ref,
    order_ref,
    src,
    tiles,
    bands,
    terms,
    first,
    centre,
    second,
    arrived,
    result,
    scalar_sem,
    src_sem,
    tile_sem,
    band_send,
    band_recv,
    term_send,
    term_recv,
    source_send,
    source_recv,
    trace_send,
    trace_recv,
    hand_send,
    hand_recv,
    go,
):
    devices = lax.axis_size("rows")
    layer, k = lax.axis_index("layer"), lax.axis_index("rows")
    shots, width = src.shape[1], src.shape[2]
    local = width // TILE
    count = tiles.shape[1]
    x, core = layer // 2, layer % 2
    partner = 1 - core
    early = x // 2

    def stage_of(d):
        return x + d * (3 - 2 * x)

    def layer_in(d):
        return core + d * (1 - 2 * core)

    def stage_core(d, at):
        return 1 - d * (at == 0).astype(jnp.int32)

    def event_of(d):
        return stage_of(d) // 2

    def is_source(d):
        return (stage_of(d) == 0) & (layer_in(d) == 0)

    def computes(d):
        return core == stage_core(d, x)

    def own_slot(d):
        inside = event_of(d) * SLOTS + jnp.where(layer_in(d) == 0, HOME, SECOND)
        return jnp.where(computes(d) & jnp.logical_not(is_source(d)), inside, OUTGOING + d)

    scalar_copies = [
        pltpu.make_async_copy(a, b, scalar_sem.at[i])
        for i, (a, b) in enumerate(
            ((rows_hbm, rows_ref), (cols_hbm, cols_ref), (order_hbm, order_ref))
        )
    ]
    src_copies = [
        pltpu.make_async_copy(ref.at[0], src.at[d], src_sem.at[d])
        for d, ref in enumerate((down_src, up_src))
    ]
    tile_copies = [
        pltpu.make_async_copy(ref.at[0], tiles.at[d], tile_sem.at[d])
        for d, ref in enumerate((down_tiles, up_tiles))
    ]

    def exists(s):
        return (k + s >= 0) & (k + s < devices)

    def present(s):
        return exists(s).astype(jnp.int32)

    barrier = pltpu.get_barrier_semaphore()

    def greet(condition, x_to, core_to, s):
        @pl.when(condition & exists(s))
        def _():
            pl.semaphore_signal(
                barrier, inc=1, device_id=(x_to * 2 + core_to, k + s), device_id_type=MESH
            )

    on_one = core == 1
    for s in (-1, 1):
        greet(on_one | (x == 0), x, partner, s)
        greet(on_one & (x >= 1), x, core, s)
    greet(True, x, partner, 0)
    for copy in scalar_copies + src_copies + tile_copies:
        copy.start()
    for s in (-2, 2, -1, 1, 0):
        greet(on_one & (x >= 1), x - 1, 1, s)
        greet((on_one & (x >= 1) & (x <= 2)) | (jnp.logical_not(on_one) & (x == 0)), x + 1, 1, s)

    for e in range(2):
        for s in (-2, -1, 1, 2):

            @pl.when(jnp.logical_not(exists(s)))
            def _():
                arrived[e, 2 + s] = jnp.zeros_like(arrived[e, 2 + s])

        for s in (-1, 1):

            @pl.when(jnp.logical_not(exists(s)))
            def _():
                at = e * SLOTS + 1 + s
                if e == 0:
                    first[1 + s] = jnp.zeros_like(first[1 + s])
                terms[at] = jnp.zeros_like(terms[at])
                bands[at] = jnp.zeros_like(bands[at])

    for copy in scalar_copies:
        copy.wait()
    slot_of = lax.broadcasted_iota(jnp.int32, (shots, shots), 0)
    shot_of = lax.broadcasted_iota(jnp.int32, (shots, shots), 1)
    wanted = jnp.zeros((shots, shots), jnp.int32)
    for j in range(shots):
        wanted = jnp.where(slot_of == j, order_ref[j], wanted)
    pick = (shot_of == wanted).astype(F32).astype(BF16)
    for copy in src_copies:
        copy.wait()
    for d in range(2):
        term = jnp.dot(pick, src[d], preferred_element_type=F32).astype(BF16)
        terms[own_slot(d)] = term

        @pl.when(is_source(d))
        def _():
            result[d] = term
            if d == 1:
                first[HOME] = term

    place = []
    for t in range(count):
        row = rows_ref[t] - k * local
        col = cols_ref[t] - (k - 1) * local
        place.append(row * 3 * local + col)

    steps = TILE // PART
    early_slot = jnp.where(early == 0, own_slot(0), own_slot(1))
    late_slot = jnp.where(early == 0, own_slot(1), own_slot(0))

    def build(step, carry):
        late, part = step // steps, step % steps
        sweep = (early + late) % 2
        slot = jnp.where(late == 0, early_slot, late_slot)
        lines = pl.ds(pl.multiple_of(part * PART, PART), PART)
        pieces = [tiles[sweep, t, lines, :].astype(F32) for t in range(count)]
        for r in range(local):
            for c in range(r, r + 5):
                total = jnp.zeros((PART, TILE), F32)
                for t in range(count):
                    total = total + jnp.where(place[t] == r * 3 * local + c, pieces[t], 0.0)
                at = pl.ds(pl.multiple_of(band_rows(c, r) + part * PART, PART), PART)
                bands[slot, at, :] = total.astype(BF16)
        return carry

    def build_from(start):
        for copy in tile_copies:
            copy.wait()
        lax.fori_loop(start, 2 * steps, build, 0)

    def send(source, target, send_sem, recv_sem, x_to, core_to, s):
        return pltpu.make_async_remote_copy(
            src_ref=source,
            dst_ref=target,
            send_sem=send_sem,
            recv_sem=recv_sem,
            device_id=(x_to * 2 + core_to, k + s),
            device_id_type=MESH,
        )

    def await_recv(buffer, sem):
        pltpu.make_async_remote_copy(
            src_ref=buffer,
            dst_ref=buffer,
            send_sem=hand_send.at[0],
            recv_sem=sem,
            device_id=(layer, k),
            device_id_type=MESH,
        ).wait_recv()

    start = lambda copy: copy.start()
    wait_send = lambda copy: copy.wait_send()

    def give(condition, d, act, seconds):
        for s in (0,) if seconds else (-1, 1, 0):
            remote = exists(s) if s else core != stage_core(d, x)
            kind = layer_in(d) == (1 if seconds else 0)

            @pl.when(condition & remote & kind & jnp.logical_not(is_source(d)))
            def _():
                at = own_slot(d)
                to = event_of(d) * SLOTS + (SECOND if seconds else 1 - s)
                for ref, ref_send, ref_recv in (
                    (terms, term_send, term_recv),
                    (bands, band_send, band_recv),
                ):
                    act(
                        send(
                            ref.at[at],
                            ref.at[to],
                            ref_send.at[d, 1 + s],
                            ref_recv.at[to],
                            x,
                            stage_core(d, x),
                            s,
                        )
                    )

    def sources(d, act):
        for s in (-1, 1, 0):
            remote = exists(s) if s else core != stage_core(d, x)

            @pl.when(is_source(d) & remote)
            def _():
                act(
                    send(
                        terms.at[OUTGOING + d],
                        first.at[1 - s],
                        source_send.at[1 + s],
                        source_recv.at[1 - s],
                        x,
                        stage_core(d, x),
                        s,
                    )
                )

    def forward(e, act):
        d = (early + e) % 2
        to = x + 1 - 2 * d
        for s in (-2, 2, -1, 1, 0):

            @pl.when(exists(s))
            def _():
                slot = (stage_of(d) + 1) // 2
                act(
                    send(
                        second.at[e],
                        arrived.at[slot, 2 - s],
                        trace_send.at[e, 2 + s],
                        trace_recv.at[slot, 2 - s],
                        to,
                        stage_core(d, to),
                        s,
                    )
                )

    def hand(e, d, from_second):
        return send(
            second.at[e] if from_second else centre.at[e],
            result.at[d],
            hand_send.at[e],
            hand_recv.at[d],
            x,
            partner,
            0,
        )

    origin = is_source(0) | is_source(1)

    @pl.when(jnp.logical_not(origin))
    def _():
        build_from(0)

    reach = present(-1) + present(0) + present(1)
    spread = reach + present(-2) + present(2)
    onward = (x <= 2).astype(jnp.int32) + (x >= 1).astype(jnp.int32)
    pl.semaphore_wait(barrier, reach + core * onward * spread)

    for d in range(2):
        sources(d, start)

    @pl.when(origin)
    def _():
        build_from(steps)

    for d in range(2):
        give(event_of(d) == 0, d, start, False)
    for d in range(2):
        give(True, d, start, True)

    between = (x >= 1) & (x <= 2)
    leads = between & (core == early)
    follows = between & (core != early)
    for d in range(2):
        give(leads & (event_of(d) == 0), d, wait_send, False)

    def let_go():
        pl.semaphore_signal(go, inc=1, device_id=(x * 2 + partner, k), device_id_type=MESH)

    @pl.when(leads)
    def _():
        let_go()

    @pl.when(follows)
    def _():
        pl.semaphore_wait(go, 1)

    for d in range(2):
        give(follows & (event_of(d) == 1), d, start, False)

    def event(e):
        d = (early + e) % 2
        X = stage_of(d)
        base = e * SLOTS
        ends_second = (d == 0) | (x == 0)

        def await_band(slot):
            here = exists(slot - 1)
            if slot == HOME:
                here = ends_second
            if slot == SECOND:
                here = jnp.logical_not(ends_second)

            @pl.when(here)
            def _():
                await_recv(terms.at[base + slot], term_recv.at[base + slot])
                await_recv(bands.at[base + slot], band_recv.at[base + slot])

        if e == 0:

            @pl.when(X == 0)
            def _():
                await_band(SECOND)
                total = terms[base + SECOND].astype(F32)
                for b in (1, 0, 2):

                    @pl.when(exists(b - 1) if b != 1 else d == 0)
                    def _():
                        await_recv(first.at[b], source_recv.at[b])

                    total = total + times(first[b], bands, base + SECOND, b)
                second[e] = total.astype(BF16)

        @pl.when(X >= 1)
        def _():
            for slot in (HOME, LEFT, RIGHT, SECOND):
                await_band(slot)
            sums = [terms[base + t].astype(F32) for t in range(3)]
            total = terms[base + SECOND].astype(F32)
            for block, done in ((2, ()), (1, ()), (3, (1,)), (0, (0,)), (4, (2,))):

                @pl.when(exists(block - 2))
                def _():
                    await_recv(arrived.at[e, block], trace_recv.at[e, block])

                for t in range(3):
                    b = block - t
                    if 0 <= b < 3:
                        sums[t] = sums[t] + times(arrived[e, block], bands, base + t, b)
                for t in done:
                    value = sums[t].astype(BF16)
                    if t == 1:
                        centre[e] = value

                        @pl.when(ends_second)
                        def _():
                            hand(e, d, False).start()

                    total = total + times(value, bands, base + SECOND, t)
            second[e] = total.astype(BF16)

        @pl.when(X < 3)
        def _():
            forward(e, start)

        @pl.when(ends_second)
        def _():
            result[d] = second[e]

        @pl.when(jnp.logical_not(ends_second))
        def _():
            hand(e, d, True).start()

            @pl.when(X >= 1)
            def _():
                result[d] = centre[e]

    @pl.when(on_one)
    def _():
        event(0)

    @pl.when(on_one & (x == 3))
    def _():
        let_go()

    @pl.when(jnp.logical_not(on_one) & (x == 3))
    def _():
        pl.semaphore_wait(go, 1)

    for d in range(2):
        give(((x == 0) | (x == 3)) & (event_of(d) == 1), d, start, False)

    late = on_one != (x == 0)

    @pl.when(late)
    def _():
        event(1)

    for d in range(2):

        @pl.when(jnp.logical_not(computes(d)) & jnp.logical_not(is_source(d)))
        def _():
            await_recv(result.at[d], hand_recv.at[d])

    out_ref[0] = (result[0].astype(F32) + result[1].astype(F32)).astype(BF16)

    for d in range(2):
        sources(d, wait_send)
        give(jnp.logical_not(leads & (event_of(d) == 0)), d, wait_send, False)
        give(True, d, wait_send, True)

    @pl.when(on_one)
    def _():
        forward(0, wait_send)

        @pl.when(x != 0)
        def _():
            hand(0, early, True).wait_send()

    @pl.when(late)
    def _():
        @pl.when(between)
        def _():
            forward(1, wait_send)

        hand(1, 1 - early, True).wait_send()


def shards(down_sources, up_sources, down_tiles, up_tiles, tile_rows, tile_cols, shot_order):
    shots, width = down_sources.shape[1:]
    count = down_tiles.shape[1]
    anywhere = pl.BlockSpec(memory_space=pl.ANY)
    dma = pltpu.SemaphoreType.DMA
    return pl.pallas_call(
        kernel,
        name="sweeps",
        out_shape=pltpu.VMEM(down_sources.shape, BF16),
        in_specs=[anywhere] * 7,
        out_specs=pl.BlockSpec(memory_space=pltpu.VMEM),
        scratch_shapes=[
            pltpu.SMEM((count,), jnp.int32),
            pltpu.SMEM((count,), jnp.int32),
            pltpu.SMEM(shot_order.shape, jnp.int32),
            pltpu.VMEM((2, shots, width), BF16),
            pltpu.VMEM((2, count, TILE, TILE), BF16),
            pltpu.VMEM((OUTGOING + 2, 10 * TILE, TILE), BF16),
            pltpu.VMEM((OUTGOING + 2, shots, width), BF16),
            pltpu.VMEM((3, shots, width), BF16),
            pltpu.VMEM((2, shots, width), BF16),
            pltpu.VMEM((2, shots, width), BF16),
            pltpu.VMEM((2, 5, shots, width), BF16),
            pltpu.VMEM((2, shots, width), BF16),
            dma((3,)),
            dma((2,)),
            dma((2,)),
            dma((2, 3)),
            dma((OUTGOING,)),
            dma((2, 3)),
            dma((OUTGOING,)),
            dma((3,)),
            dma((3,)),
            dma((2, 5)),
            dma((2, 5)),
            dma((2,)),
            dma((2,)),
            pltpu.SemaphoreType.REGULAR,
        ],
        compiler_params=pltpu.CompilerParams(collective_id=0, has_side_effects=True),
    )(tile_rows[0], tile_cols[0], shot_order, down_sources, up_sources, down_tiles, up_tiles)


def solution(mesh):
    return jax.shard_map(
        shards,
        mesh=mesh,
        in_specs=(
            P("layer", None, "rows"),
            P("layer", None, "rows"),
            P("layer", "rows", None, None),
            P("layer", "rows", None, None),
            P("layer", "rows"),
            P("layer", "rows"),
            P(),
        ),
        out_specs=P("layer", None, "rows"),
        check_vma=False,
    )
```

```python
import jax
import jax.numpy as jnp
from jax import lax
from jax.experimental import pallas as pl
from jax.experimental.pallas import tpu as pltpu
from jax.sharding import PartitionSpec as P

TILE = 128
MESH = pl.DeviceIdType.MESH
F32 = jnp.float32
BF16 = jnp.bfloat16
LEFT, HOME, RIGHT, SECOND = range(4)
SLOTS = 4
OUTGOING = 2 * SLOTS
PART = 16
PLANE = 4


REACH = 5 * TILE


def band_rows(c, r):
    return r * REACH + (c - r) * TILE


def band_block(bands, slot, b):
    def tile(c, r):
        return bands[slot, pl.ds(band_rows(c, r), TILE), :]

    def line(r):
        pieces = [
            tile(c, r) if abs(c - 2 - r) <= 2 else jnp.zeros((TILE, TILE), BF16)
            for c in (2 * b, 2 * b + 1)
        ]
        return jnp.concatenate(pieces, axis=1)

    return jnp.concatenate([line(0), line(1)], axis=0)


def times(block, bands, slot, b):
    return lax.dot_general(
        block, band_block(bands, slot, b), (((1,), (1,)), ((), ())), preferred_element_type=F32
    )


def kernel(
    rows_hbm,
    cols_hbm,
    order_hbm,
    down_src,
    up_src,
    down_tiles,
    up_tiles,
    out_ref,
    rows_ref,
    cols_ref,
    order_ref,
    src,
    tiles,
    bands,
    terms,
    first,
    centre,
    second,
    arrived,
    beside,
    products,
    result,
    scalar_sem,
    src_sem,
    tile_sem,
    band_send,
    band_recv,
    term_send,
    term_recv,
    source_send,
    source_recv,
    trace_send,
    trace_recv,
    beside_send,
    beside_recv,
    hand_send,
    hand_recv,
    go,
):
    devices = lax.axis_size("rows")
    layer, k = lax.axis_index("layer"), lax.axis_index("rows")
    shots, width = src.shape[1], src.shape[2]
    local = width // TILE
    count = tiles.shape[1]
    x, core = layer // 2, layer % 2
    partner = 1 - core
    early = x // 2

    def stage_of(d):
        return x + d * (3 - 2 * x)

    def layer_in(d):
        return core + d * (1 - 2 * core)

    def stage_core(d, at):
        return 1 - d * (at == 0).astype(jnp.int32)

    def event_of(d):
        return stage_of(d) // 2

    def is_source(d):
        return (stage_of(d) == 0) & (layer_in(d) == 0)

    def computes(d):
        return core == stage_core(d, x)

    def own_slot(d):
        inside = event_of(d) * SLOTS + jnp.where(layer_in(d) == 0, HOME, SECOND)
        return jnp.where(computes(d) & jnp.logical_not(is_source(d)), inside, OUTGOING + d)

    scalar_copies = [
        pltpu.make_async_copy(a, b, scalar_sem.at[i])
        for i, (a, b) in enumerate(
            ((rows_hbm, rows_ref), (cols_hbm, cols_ref), (order_hbm, order_ref))
        )
    ]
    src_copies = [
        pltpu.make_async_copy(ref.at[0], src.at[d], src_sem.at[d])
        for d, ref in enumerate((down_src, up_src))
    ]
    tile_copies = [
        pltpu.make_async_copy(ref.at[0], tiles.at[d], tile_sem.at[d])
        for d, ref in enumerate((down_tiles, up_tiles))
    ]

    def exists(s):
        return (k + s >= 0) & (k + s < devices)

    def present(s):
        return exists(s).astype(jnp.int32)

    barrier = pltpu.get_barrier_semaphore()

    def greet(condition, x_to, core_to, s):
        @pl.when(condition & exists(s))
        def _():
            pl.semaphore_signal(
                barrier, inc=1, device_id=(x_to * 2 + core_to, k + s), device_id_type=MESH
            )

    on_one = core == 1
    for s in (-1, 1):
        greet(on_one | (x == 0), x, partner, s)
        greet(on_one & (x >= 1), x, core, s)
    greet(True, x, partner, 0)
    for copy in scalar_copies + src_copies + tile_copies:
        copy.start()
    for s in (-2, 2, -1, 1, 0):
        greet(on_one & (x >= 1), x - 1, 1, s)
        greet((on_one & (x >= 1) & (x <= 2)) | (jnp.logical_not(on_one) & (x == 0)), x + 1, 1, s)
    tail = jnp.where(x == 0, on_one, jnp.logical_not(on_one) & (x == 3))
    for s in (-1, 1, 0):
        greet(tail, jnp.where(x == 0, x + 1, x - 1), 1, s)

    for e in range(2):
        for s in (-2, -1, 1, 2):

            @pl.when(jnp.logical_not(exists(s)))
            def _():
                arrived[e, 2 + s] = jnp.zeros_like(arrived[e, 2 + s])

        for s in (-1, 1):

            @pl.when(jnp.logical_not(exists(s)))
            def _():
                at = e * SLOTS + 1 + s
                if e == 0:
                    first[1 + s] = jnp.zeros_like(first[1 + s])
                    beside[1 + s] = jnp.zeros_like(beside[1 + s])
                terms[at] = jnp.zeros_like(terms[at])
                bands[at] = jnp.zeros_like(bands[at])

    for copy in scalar_copies:
        copy.wait()
    slot_of = lax.broadcasted_iota(jnp.int32, (shots, shots), 0)
    shot_of = lax.broadcasted_iota(jnp.int32, (shots, shots), 1)
    wanted = jnp.zeros((shots, shots), jnp.int32)
    for j in range(shots):
        wanted = jnp.where(slot_of == j, order_ref[j], wanted)
    pick = (shot_of == wanted).astype(F32).astype(BF16)
    for copy in src_copies:
        copy.wait()
    for d in range(2):
        term = jnp.dot(pick, src[d], preferred_element_type=F32).astype(BF16)
        terms[own_slot(d)] = term

        @pl.when(is_source(d))
        def _():
            result[d] = term
            if d == 1:
                first[HOME] = term

    place = []
    for t in range(count):
        row = rows_ref[t] - k * local
        col = cols_ref[t] - (k - 1) * local
        place.append(row * 3 * local + col)

    steps = TILE // PART
    early_slot = jnp.where(early == 0, own_slot(0), own_slot(1))
    late_slot = jnp.where(early == 0, own_slot(1), own_slot(0))

    def build(late, r):
        sweep = (early + late) % 2
        slot = late_slot if late else early_slot

        def step(part, carry):
            lines = pl.ds(pl.multiple_of(part * PART, PART), PART)
            pieces = [tiles[sweep, t, lines, :].astype(F32) for t in range(count)]
            for c in range(r, r + 5):
                total = jnp.zeros((PART, TILE), F32)
                for t in range(count):
                    total = total + jnp.where(place[t] == r * 3 * local + c, pieces[t], 0.0)
                at = pl.ds(pl.multiple_of(band_rows(c, r) + part * PART, PART), PART)
                bands[slot, at, :] = total.astype(BF16)
            return carry

        lax.fori_loop(0, steps, step, 0)

    def send(source, target, send_sem, recv_sem, x_to, core_to, s):
        return pltpu.make_async_remote_copy(
            src_ref=source,
            dst_ref=target,
            send_sem=send_sem,
            recv_sem=recv_sem,
            device_id=(x_to * 2 + core_to, k + s),
            device_id_type=MESH,
        )

    def await_recv(buffer, sem):
        pltpu.make_async_remote_copy(
            src_ref=buffer,
            dst_ref=buffer,
            send_sem=hand_send.at[0],
            recv_sem=sem,
            device_id=(layer, k),
            device_id_type=MESH,
        ).wait_recv()

    start = lambda copy: copy.start()
    wait_send = lambda copy: copy.wait_send()

    def give(condition, d, act, seconds, terms_too=True, lines=(0, 1)):
        for s in (0,) if seconds else (-1, 1, 0):
            remote = exists(s) if s else core != stage_core(d, x)
            kind = layer_in(d) == (1 if seconds else 0)

            @pl.when(condition & remote & kind & jnp.logical_not(is_source(d)))
            def _():
                at = own_slot(d)
                to = event_of(d) * SLOTS + (SECOND if seconds else 1 - s)
                there = (x, stage_core(d, x), s)
                if terms_too:
                    act(
                        send(
                            terms.at[at],
                            terms.at[to],
                            term_send.at[d, 1 + s],
                            term_recv.at[to],
                            *there,
                        )
                    )
                for r in lines:
                    piece = pl.ds(r * REACH, REACH)
                    act(
                        send(
                            bands.at[at, piece],
                            bands.at[to, piece],
                            band_send.at[d, 1 + s, r],
                            band_recv.at[to, r],
                            *there,
                        )
                    )

    def sources(d, act):
        for s in (-1, 1, 0):
            remote = exists(s) if s else core != stage_core(d, x)

            @pl.when(is_source(d) & remote)
            def _():
                act(
                    send(
                        terms.at[OUTGOING + d],
                        first.at[1 - s],
                        source_send.at[1 + s],
                        source_recv.at[1 - s],
                        x,
                        stage_core(d, x),
                        s,
                    )
                )

    def forward(e, act):
        d = (early + e) % 2
        to = x + 1 - 2 * d
        slot = (stage_of(d) + 1) // 2

        def main(s):
            return send(
                second.at[e],
                arrived.at[slot, 2 - s],
                trace_send.at[e, 2 + s],
                trace_recv.at[slot, 2 - s],
                to,
                stage_core(d, to),
                s,
            )

        def extra(s):
            return send(
                second.at[e],
                beside.at[1 - s],
                beside_send.at[1 + s],
                beside_recv.at[1 - s],
                to,
                1 - stage_core(d, to),
                s,
            )

        for far in (True, False):
            for copies, reached in ((main, (-1, 1, -2, 2, 0)), (extra, (-1, 1, 0))):
                if copies is extra and e == 0:
                    continue
                for s in reached:
                    if far and s == 0:
                        continue
                    side = (k % PLANE + s) // PLANE != 0

                    @pl.when(exists(s) & (side if far else jnp.logical_not(side)))
                    def _():
                        act(copies(s))

    def hand(e, d, from_second):
        return send(
            second.at[e] if from_second else centre.at[e],
            result.at[d],
            hand_send.at[e],
            hand_recv.at[d],
            x,
            partner,
            0,
        )

    origin = is_source(0) | is_source(1)

    for copy in tile_copies:
        copy.wait()

    @pl.when(jnp.logical_not(origin))
    def _():
        build(0, 0)

    reach = present(-1) + present(0) + present(1)
    spread = reach + present(-2) + present(2)
    onward = (x <= 2).astype(jnp.int32) + (x >= 1).astype(jnp.int32)
    between = (x >= 1) & (x <= 2)
    pl.semaphore_wait(
        barrier,
        reach + core * (onward * spread + between.astype(jnp.int32) * reach),
    )

    for d in range(2):
        sources(d, start)
    for d in range(2):
        for seconds in (False, True):
            give(event_of(d) == 0, d, start, seconds, True, (0,))

    @pl.when(jnp.logical_not(origin))
    def _():
        build(0, 1)

    for d in range(2):
        for seconds in (False, True):
            give(event_of(d) == 0, d, start, seconds, False, (1,))
    for r in range(2):
        build(1, r)
    for d in range(2):
        give(event_of(d) == 1, d, start, True)

    def let_go():
        pl.semaphore_signal(go, inc=1, device_id=(x * 2 + partner, k), device_id_type=MESH)

    leads = between & (core == early)
    follows = between & (core != early)
    for d in range(2):
        give(leads & (event_of(d) == 0), d, wait_send, False, False, (0,))

    @pl.when(leads)
    def _():
        let_go()

    @pl.when(follows)
    def _():
        pl.semaphore_wait(go, 1)

    for d in range(2):
        give(follows & (event_of(d) == 1), d, start, False)

    def event(e):
        d = (early + e) % 2
        X = stage_of(d)
        base = e * SLOTS
        ends_second = (d == 0) | (x == 0)

        def await_band(slot):
            here = exists(slot - 1)
            if slot == HOME:
                here = ends_second
            if slot == SECOND:
                here = jnp.logical_not(ends_second)

            @pl.when(here)
            def _():
                await_recv(terms.at[base + slot], term_recv.at[base + slot])
                for r in range(2):
                    piece = bands.at[base + slot, pl.ds(r * REACH, REACH)]
                    await_recv(piece, band_recv.at[base + slot, r])

        if e == 0:

            @pl.when(X == 0)
            def _():
                await_band(SECOND)
                total = terms[base + SECOND].astype(F32)
                for b in (1, 0, 2):

                    @pl.when(exists(b - 1) if b != 1 else d == 0)
                    def _():
                        await_recv(first.at[b], source_recv.at[b])

                    total = total + times(first[b], bands, base + SECOND, b)
                second[e] = total.astype(BF16)

        def await_block(block):
            @pl.when((k + block - 2 >= 0) & (k + block - 2 < devices))
            def _():
                await_recv(arrived.at[e, block], trace_recv.at[e, block])

        if e == 0:

            @pl.when(X >= 1)
            def _():
                for slot in (HOME, LEFT, RIGHT, SECOND):
                    await_band(slot)
                sums = [terms[base + t].astype(F32) for t in range(3)]
                total = terms[base + SECOND].astype(F32)
                for block, done in ((2, ()), (1, ()), (3, (1,)), (0, (0,)), (4, (2,))):
                    await_block(block)
                    for t in range(3):
                        b = block - t
                        if 0 <= b < 3:
                            sums[t] = sums[t] + times(arrived[e, block], bands, base + t, b)
                    for t in done:
                        value = sums[t].astype(BF16)
                        if t == 1:
                            centre[e] = value
                        total = total + times(value, bands, base + SECOND, t)
                second[e] = total.astype(BF16)

            forward(e, start)

            @pl.when(X >= 1)
            def _():
                @pl.when(ends_second)
                def _():
                    hand(e, d, False).start()

        else:
            for slot in (HOME, LEFT, RIGHT, SECOND):
                await_band(slot)
            total = terms[base + SECOND].astype(F32)
            outer = [band_block(bands, base + SECOND, t) for t in range(3)]
            for t in range(3):
                total = total + times(terms[base + t], bands, base + SECOND, t)
            for block in range(5):
                product = None
                for t in range(3):
                    b = block - t
                    if 0 <= b < 3:
                        part = jnp.dot(
                            outer[t], band_block(bands, base + t, b), preferred_element_type=F32
                        )
                        product = part if product is None else product + part
                products[block] = product.astype(BF16)
            turn = 1 - 2 * (k % PLANE >= PLANE // 2).astype(jnp.int32)
            for j in (0, 1, 2, -1, -2):
                block = 2 + j * turn
                await_block(block)
                total = total + lax.dot_general(
                    arrived[e, block],
                    products[block],
                    (((1,), (1,)), ((), ())),
                    preferred_element_type=F32,
                )
            second[e] = total.astype(BF16)

            @pl.when(X < 3)
            def _():
                forward(e, start)
                inner = terms[base + HOME].astype(F32)
                for b in range(3):
                    inner = inner + times(arrived[e, 1 + b], bands, base + HOME, b)
                centre[e] = inner.astype(BF16)

                @pl.when(ends_second)
                def _():
                    hand(e, d, False).start()

        @pl.when(ends_second)
        def _():
            result[d] = second[e]

        @pl.when(jnp.logical_not(ends_second))
        def _():
            hand(e, d, True).start()

            @pl.when(X >= 1)
            def _():
                result[d] = centre[e]

    @pl.when(on_one)
    def _():
        event(0)

    @pl.when(on_one & (x == 3))
    def _():
        let_go()

    @pl.when(jnp.logical_not(on_one) & (x == 3))
    def _():
        pl.semaphore_wait(go, 1)

    for d in range(2):
        give(((x == 0) | (x == 3)) & (event_of(d) == 1), d, start, False)

    late = on_one != (x == 0)

    def finish():
        for d in range(2):
            sources(d, wait_send)
            led = leads & (event_of(d) == 0)
            give(led, d, wait_send, False, True, (1,))
            give(jnp.logical_not(led), d, wait_send, False)
            give(True, d, wait_send, True)

        @pl.when(on_one)
        def _():
            forward(0, wait_send)

            @pl.when(x != 0)
            def _():
                hand(0, early, True).wait_send()

    @pl.when(jnp.logical_not(between))
    def _():
        finish()

    @pl.when(late)
    def _():
        event(1)

    for d in range(2):
        last = stage_of(d) == 3

        @pl.when(tail & last)
        def _():
            at = OUTGOING + d
            total = terms[at].astype(F32)
            for b in (1, 0, 2):

                @pl.when(exists(b - 1))
                def _():
                    await_recv(beside.at[b], beside_recv.at[b])

                total = total + times(beside[b], bands, at, b)
            result[d] = total.astype(BF16)

        @pl.when(jnp.logical_not(computes(d) | is_source(d) | last))
        def _():
            await_recv(result.at[d], hand_recv.at[d])

    out_ref[0] = (result[0].astype(F32) + result[1].astype(F32)).astype(BF16)

    @pl.when(between)
    def _():
        finish()

        @pl.when(late)
        def _():
            forward(1, wait_send)
            hand(1, 1 - early, True).wait_send()


def shards(down_sources, up_sources, down_tiles, up_tiles, tile_rows, tile_cols, shot_order):
    shots, width = down_sources.shape[1:]
    count = down_tiles.shape[1]
    anywhere = pl.BlockSpec(memory_space=pl.ANY)
    dma = pltpu.SemaphoreType.DMA
    return pl.pallas_call(
        kernel,
        name="sweeps",
        out_shape=pltpu.VMEM(down_sources.shape, BF16),
        in_specs=[anywhere] * 7,
        out_specs=pl.BlockSpec(memory_space=pltpu.VMEM),
        scratch_shapes=[
            pltpu.SMEM((count,), jnp.int32),
            pltpu.SMEM((count,), jnp.int32),
            pltpu.SMEM(shot_order.shape, jnp.int32),
            pltpu.VMEM((2, shots, width), BF16),
            pltpu.VMEM((2, count, TILE, TILE), BF16),
            pltpu.VMEM((OUTGOING + 2, 10 * TILE, TILE), BF16),
            pltpu.VMEM((OUTGOING + 2, shots, width), BF16),
            pltpu.VMEM((3, shots, width), BF16),
            pltpu.VMEM((2, shots, width), BF16),
            pltpu.VMEM((2, shots, width), BF16),
            pltpu.VMEM((2, 5, shots, width), BF16),
            pltpu.VMEM((3, shots, width), BF16),
            pltpu.VMEM((5, width, width), BF16),
            pltpu.VMEM((2, shots, width), BF16),
            dma((3,)),
            dma((2,)),
            dma((2,)),
            dma((2, 3, 2)),
            dma((OUTGOING, 2)),
            dma((2, 3)),
            dma((OUTGOING,)),
            dma((3,)),
            dma((3,)),
            dma((2, 5)),
            dma((2, 5)),
            dma((3,)),
            dma((3,)),
            dma((2,)),
            dma((2,)),
            pltpu.SemaphoreType.REGULAR,
        ],
        compiler_params=pltpu.CompilerParams(collective_id=0, has_side_effects=True),
    )(tile_rows[0], tile_cols[0], shot_order, down_sources, up_sources, down_tiles, up_tiles)


def solution(mesh):
    return jax.shard_map(
        shards,
        mesh=mesh,
        in_specs=(
            P("layer", None, "rows"),
            P("layer", None, "rows"),
            P("layer", "rows", None, None),
            P("layer", "rows", None, None),
            P("layer", "rows"),
            P("layer", "rows"),
            P(),
        ),
        out_specs=P("layer", None, "rows"),
        check_vma=False,
    )
```

```python
import jax
import jax.numpy as jnp
from jax import lax
from jax.experimental import pallas as pl
from jax.experimental.pallas import tpu as pltpu
from jax.sharding import PartitionSpec as P

TILE = 128
MESH = pl.DeviceIdType.MESH
F32 = jnp.float32
BF16 = jnp.bfloat16
LEFT, HOME, RIGHT, SECOND = range(4)
SLOTS = 4
OUTGOING = 2 * SLOTS
PART = 16
PLANE = 4


REACH = 5 * TILE
TERM = 64


def band_rows(c, r):
    return r * REACH + (c - r) * TILE


def band_block(bands, slot, b):
    def tile(c, r):
        return bands[slot, pl.ds(band_rows(c, r), TILE), :]

    def line(r):
        pieces = [
            tile(c, r) if abs(c - 2 - r) <= 2 else jnp.zeros((TILE, TILE), BF16)
            for c in (2 * b, 2 * b + 1)
        ]
        return jnp.concatenate(pieces, axis=1)

    return jnp.concatenate([line(0), line(1)], axis=0)


def times(block, bands, slot, b):
    return lax.dot_general(
        block, band_block(bands, slot, b), (((1,), (1,)), ((), ())), preferred_element_type=F32
    )


def kernel(
    rows_hbm,
    cols_hbm,
    order_hbm,
    down_src,
    up_src,
    down_tiles,
    up_tiles,
    out_ref,
    rows_ref,
    cols_ref,
    order_ref,
    src,
    tiles,
    bands,
    terms,
    first,
    centre,
    second,
    arrived,
    beside,
    products,
    result,
    scalar_sem,
    src_sem,
    tile_sem,
    band_send,
    band_recv,
    side_send,
    trace_send,
    trace_recv,
    hand_send,
    hand_recv,
    go,
    far,
):
    devices = lax.axis_size("rows")
    layer, k = lax.axis_index("layer"), lax.axis_index("rows")
    shots, width = src.shape[1], src.shape[2]
    local = width // TILE
    count = tiles.shape[1]
    x, core = layer // 2, layer % 2
    partner = 1 - core
    early = x // 2

    def stage_of(d):
        return x + d * (3 - 2 * x)

    def layer_in(d):
        return core + d * (1 - 2 * core)

    def stage_core(d, at):
        return 1 - d * (at == 0).astype(jnp.int32)

    def event_of(d):
        return stage_of(d) // 2

    def is_source(d):
        return (stage_of(d) == 0) & (layer_in(d) == 0)

    def computes(d):
        return core == stage_core(d, x)

    def own_slot(d):
        inside = event_of(d) * SLOTS + jnp.where(layer_in(d) == 0, HOME, SECOND)
        return jnp.where(computes(d) & jnp.logical_not(is_source(d)), inside, OUTGOING + d)

    scalar_copies = [
        pltpu.make_async_copy(a, b, scalar_sem.at[i])
        for i, (a, b) in enumerate(
            ((rows_hbm, rows_ref), (cols_hbm, cols_ref), (order_hbm, order_ref))
        )
    ]
    src_copies = [
        pltpu.make_async_copy(ref.at[0], src.at[d], src_sem)
        for d, ref in enumerate((down_src, up_src))
    ]
    tile_copies = [
        pltpu.make_async_copy(ref.at[0], tiles.at[d], tile_sem)
        for d, ref in enumerate((down_tiles, up_tiles))
    ]

    def exists(s):
        return (k + s >= 0) & (k + s < devices)

    def present(s):
        return exists(s).astype(jnp.int32)

    barrier = pltpu.get_barrier_semaphore()

    def greet(condition, x_to, core_to, s):
        @pl.when(condition & exists(s))
        def _():
            pl.semaphore_signal(
                barrier, inc=1, device_id=(x_to * 2 + core_to, k + s), device_id_type=MESH
            )

    on_one = core == 1
    for s in (-1, 1):
        greet(on_one | (x == 0), x, partner, s)
        greet(on_one & (x >= 1), x, core, s)
    greet(True, x, partner, 0)
    for copy in scalar_copies + src_copies + tile_copies:
        copy.start()
    def collector(x_to):
        return (x_to <= 1).astype(jnp.int32)

    for s in (-2, 2, -1, 1, 0):
        greet(on_one & (x >= 1), x - 1, collector(x - 1), s)
        onto = (on_one & (x >= 1) & (x <= 2)) | (jnp.logical_not(on_one) & (x == 0))
        greet(onto, x + 1, collector(x + 1), s)
    tail = jnp.where(x == 0, on_one, jnp.logical_not(on_one) & (x == 3))
    for s in (-1, 1, 0):
        to = jnp.where(x == 0, x + 1, x - 1)
        greet(tail, to, collector(to), s)

    for e in range(2):
        for s in (-2, -1, 1, 2):

            @pl.when(jnp.logical_not(exists(s)))
            def _():
                arrived[e, 2 + s] = jnp.zeros_like(arrived[e, 2 + s])

        for s in (-1, 1):

            @pl.when(jnp.logical_not(exists(s)))
            def _():
                at = e * SLOTS + 1 + s
                if e == 0:
                    first[1 + s] = jnp.zeros_like(first[1 + s])
                    beside[1 + s] = jnp.zeros_like(beside[1 + s])
                terms[at] = jnp.zeros_like(terms[at])
                bands[at] = jnp.zeros_like(bands[at])

    for copy in scalar_copies:
        copy.wait()
    slot_of = lax.broadcasted_iota(jnp.int32, (shots, shots), 0)
    shot_of = lax.broadcasted_iota(jnp.int32, (shots, shots), 1)
    wanted = jnp.zeros((shots, shots), jnp.int32)
    for j in range(shots):
        wanted = jnp.where(slot_of == j, order_ref[j], wanted)
    pick = (shot_of == wanted).astype(F32).astype(BF16)
    pltpu.make_async_copy(src, src, src_sem).wait()
    for d in range(2):
        term = jnp.dot(pick, src[d], preferred_element_type=F32).astype(BF16)
        terms[own_slot(d)] = term

        @pl.when(is_source(d))
        def _():
            result[d] = term
            if d == 1:
                first[HOME] = term

    place = []
    for t in range(count):
        row = rows_ref[t] - k * local
        col = cols_ref[t] - (k - 1) * local
        place.append(row * 3 * local + col)

    steps = TILE // PART
    early_slot = jnp.where(early == 0, own_slot(0), own_slot(1))
    late_slot = jnp.where(early == 0, own_slot(1), own_slot(0))

    def build(late, r):
        sweep = (early + late) % 2
        slot = late_slot if late else early_slot

        def step(part, carry):
            lines = pl.ds(pl.multiple_of(part * PART, PART), PART)
            pieces = [tiles[sweep, t, lines, :].astype(F32) for t in range(count)]
            for c in range(r, r + 5):
                total = jnp.zeros((PART, TILE), F32)
                for t in range(count):
                    total = total + jnp.where(place[t] == r * 3 * local + c, pieces[t], 0.0)
                at = pl.ds(pl.multiple_of(band_rows(c, r) + part * PART, PART), PART)
                bands[slot, at, :] = total.astype(BF16)
            return carry

        lax.fori_loop(0, steps, step, 0)

    def send(source, target, send_sem, recv_sem, x_to, core_to, s):
        return pltpu.make_async_remote_copy(
            src_ref=source,
            dst_ref=target,
            send_sem=send_sem,
            recv_sem=recv_sem,
            device_id=(x_to * 2 + core_to, k + s),
            device_id_type=MESH,
        )

    def await_recv(buffer, sem):
        pltpu.make_async_remote_copy(
            src_ref=buffer,
            dst_ref=buffer,
            send_sem=hand_send.at[0],
            recv_sem=sem,
            device_id=(layer, k),
            device_id_type=MESH,
        ).wait_recv()

    start = lambda copy: copy.start()
    wait_send = lambda copy: copy.wait_send()

    def give(condition, d, act, seconds, lines=(0, 1)):
        for s in (0,) if seconds else (-1, 1, 0):
            remote = exists(s) if s else core != stage_core(d, x)
            kind = layer_in(d) == (1 if seconds else 0)

            @pl.when(condition & remote & kind & jnp.logical_not(is_source(d)))
            def _():
                at = own_slot(d)
                to = event_of(d) * SLOTS + (SECOND if seconds else 1 - s)
                lane = 3 if seconds else 1 + s

                def part(source, target, r):
                    return send(
                        source,
                        target,
                        band_send.at[lane, r],
                        band_recv.at[to, r],
                        x,
                        stage_core(d, x),
                        s,
                    )

                for r in lines:
                    if act is wait_send:
                        both = bands.at[at, pl.ds(0, REACH + r * TERM)]
                        part(both, both, r).wait_send()
                        continue
                    piece = pl.ds(r * REACH, REACH)
                    act(part(bands.at[at, piece], bands.at[to, piece], r))
                    if r == 1:
                        act(part(terms.at[at], terms.at[to], r))

    def sources(d, act):
        for s in (-1, 1, 0):
            remote = exists(s) if s else core != stage_core(d, x)

            @pl.when(is_source(d) & remote)
            def _():
                act(
                    send(
                        terms.at[OUTGOING + d],
                        first.at[1 - s],
                        side_send.at[1 + s],
                        trace_recv.at[0, 2 - s],
                        x,
                        stage_core(d, x),
                        s,
                    )
                )

    def forward(e, act):
        d = (early + e) % 2
        to = x + 1 - 2 * d
        slot = (stage_of(d) + 1) // 2

        def main(s):
            return send(
                second.at[e],
                arrived.at[slot, 2 - s],
                trace_send.at[e],
                trace_recv.at[slot, 2 - s],
                to,
                stage_core(d, to),
                s,
            )

        def extra(s):
            return send(
                second.at[e],
                beside.at[1 - s],
                side_send.at[1 + s],
                trace_recv.at[1, 2 - s],
                to,
                1 - stage_core(d, to),
                s,
            )

        if act is wait_send:
            for n in (3, 4, 5):

                @pl.when(spread == n)
                def _():
                    blocks = arrived.at[0, pl.ds(0, n)]
                    send(blocks, blocks, trace_send.at[e], trace_recv.at[0, 0], x, partner, 0).wait_send()

            if e == 1:
                for s in (-1, 1, 0):

                    @pl.when(exists(s))
                    def _():
                        extra(s).wait_send()

            return

        for crossing in (True, False):
            for copies, reached in ((main, (-1, 1, -2, 2, 0)), (extra, (-1, 1, 0))):
                if copies is extra and e == 0:
                    continue
                for s in reached:
                    if crossing and s == 0:
                        continue
                    side = (k % PLANE + s) // PLANE != 0

                    @pl.when(exists(s) & (side if crossing else jnp.logical_not(side)))
                    def _():
                        act(copies(s))

    def hand(e, d, from_second):
        return send(
            second.at[e] if from_second else centre.at[e],
            result.at[d],
            hand_send.at[e],
            hand_recv.at[d],
            x,
            partner,
            0,
        )

    origin = is_source(0) | is_source(1)

    pltpu.make_async_copy(tiles, tiles, tile_sem).wait()

    @pl.when(jnp.logical_not(origin))
    def _():
        build(0, 0)

    patient = jnp.logical_not(on_one) & (x >= 2)

    @pl.when(patient)
    def _():
        build(0, 1)

    reach = present(-1) + present(0) + present(1)
    spread = reach + present(-2) + present(2)
    onward = (x <= 2).astype(jnp.int32) + (x >= 1).astype(jnp.int32)
    between = (x >= 1) & (x <= 2)
    collects = core == collector(x)
    pl.semaphore_wait(
        barrier,
        reach
        + collects.astype(jnp.int32) * (onward * spread + between.astype(jnp.int32) * reach),
    )

    @pl.when(collects & (x >= 2))
    def _():
        pl.semaphore_signal(far, inc=1, device_id=(x * 2 + partner, k), device_id_type=MESH)

    for d in range(2):
        sources(d, start)
    for d in range(2):
        for seconds in (False, True):
            give(event_of(d) == 0, d, start, seconds, (0,))

    @pl.when(jnp.logical_not(origin | patient))
    def _():
        build(0, 1)

    for d in range(2):
        for seconds in (False, True):
            give(event_of(d) == 0, d, start, seconds, (1,))
    for r in range(2):
        build(1, r)
    for d in range(2):
        give(event_of(d) == 1, d, start, True)

    def let_go():
        pl.semaphore_signal(go, inc=1, device_id=(x * 2 + partner, k), device_id_type=MESH)

    leads = between & (core == early)
    follows = between & (core != early)
    for d in range(2):
        give(leads & (event_of(d) == 0), d, wait_send, False, (0,))

    @pl.when(leads)
    def _():
        let_go()

    @pl.when(follows)
    def _():
        pl.semaphore_wait(go, 1)

    for d in range(2):
        give(follows & (event_of(d) == 1), d, start, False)

    def event(e):
        d = (early + e) % 2
        X = stage_of(d)
        base = e * SLOTS
        ends_second = (d == 0) | (x == 0)

        def await_band(slot):
            here = exists(slot - 1)
            if slot == HOME:
                here = ends_second
            if slot == SECOND:
                here = jnp.logical_not(ends_second)

            @pl.when(here)
            def _():
                for r in range(2):
                    piece = bands.at[base + slot, pl.ds(0, REACH + r * TERM)]
                    await_recv(piece, band_recv.at[base + slot, r])

        if e == 0:

            @pl.when(X == 0)
            def _():
                await_band(SECOND)
                total = terms[base + SECOND].astype(F32)
                for b in (1, 0, 2):

                    @pl.when(exists(b - 1) if b != 1 else d == 0)
                    def _():
                        await_recv(first.at[b], trace_recv.at[0, 1 + b])

                    total = total + times(first[b], bands, base + SECOND, b)
                second[e] = total.astype(BF16)

        def await_block(block):
            @pl.when((k + block - 2 >= 0) & (k + block - 2 < devices))
            def _():
                await_recv(arrived.at[e, block], trace_recv.at[e, block])

        if e == 0:

            @pl.when(X >= 1)
            def _():
                for slot in (HOME, LEFT, RIGHT, SECOND):
                    await_band(slot)
                sums = [terms[base + t].astype(F32) for t in range(3)]
                total = terms[base + SECOND].astype(F32)
                for block, done in ((2, ()), (1, ()), (3, (1,)), (0, (0,)), (4, (2,))):
                    await_block(block)
                    for t in range(3):
                        b = block - t
                        if 0 <= b < 3:
                            sums[t] = sums[t] + times(arrived[e, block], bands, base + t, b)
                    for t in done:
                        value = sums[t].astype(BF16)
                        if t == 1:
                            centre[e] = value
                        total = total + times(value, bands, base + SECOND, t)
                second[e] = total.astype(BF16)

            @pl.when(x >= 2)
            def _():
                pl.semaphore_wait(far, 1)

            forward(e, start)

            @pl.when(X >= 1)
            def _():
                @pl.when(ends_second)
                def _():
                    hand(e, d, False).start()

        else:
            for slot in (HOME, LEFT, RIGHT, SECOND):
                await_band(slot)
            total = terms[base + SECOND].astype(F32)
            outer = [band_block(bands, base + SECOND, t) for t in range(3)]
            for t in range(3):
                total = total + times(terms[base + t], bands, base + SECOND, t)
            for block in range(5):
                product = None
                for t in range(3):
                    b = block - t
                    if 0 <= b < 3:
                        part = jnp.dot(
                            outer[t], band_block(bands, base + t, b), preferred_element_type=F32
                        )
                        product = part if product is None else product + part
                products[block] = product.astype(BF16)
            turn = 1 - 2 * (k % PLANE >= PLANE // 2).astype(jnp.int32)
            for j in (0, 1, 2, -1, -2):
                block = 2 + j * turn
                await_block(block)
                total = total + lax.dot_general(
                    arrived[e, block],
                    products[block],
                    (((1,), (1,)), ((), ())),
                    preferred_element_type=F32,
                )
            second[e] = total.astype(BF16)

            @pl.when(X < 3)
            def _():
                forward(e, start)
                inner = terms[base + HOME].astype(F32)
                for b in range(3):
                    inner = inner + times(arrived[e, 1 + b], bands, base + HOME, b)
                centre[e] = inner.astype(BF16)

                @pl.when(ends_second)
                def _():
                    hand(e, d, False).start()

        @pl.when(ends_second)
        def _():
            result[d] = second[e]

        @pl.when(jnp.logical_not(ends_second))
        def _():
            hand(e, d, True).start()

            @pl.when(X >= 1)
            def _():
                result[d] = centre[e]

    @pl.when(on_one)
    def _():
        event(0)

    @pl.when(on_one & (x == 3))
    def _():
        let_go()

    @pl.when(jnp.logical_not(on_one) & (x == 3))
    def _():
        pl.semaphore_wait(go, 1)

    for d in range(2):
        give(((x == 0) | (x == 3)) & (event_of(d) == 1), d, start, False)

    late = on_one != (x == 0)

    def finish():
        for d in range(2):
            sources(d, wait_send)
            led = leads & (event_of(d) == 0)
            give(led, d, wait_send, False, (1,))
            give(jnp.logical_not(led), d, wait_send, False)
            give(True, d, wait_send, True)

        @pl.when(on_one)
        def _():
            forward(0, wait_send)

            @pl.when(x != 0)
            def _():
                hand(0, early, True).wait_send()

    @pl.when(jnp.logical_not(between))
    def _():
        finish()

    @pl.when(late)
    def _():
        event(1)

    for d in range(2):
        last = stage_of(d) == 3

        @pl.when(tail & last)
        def _():
            at = OUTGOING + d
            total = terms[at].astype(F32)
            for b in (1, 0, 2):

                @pl.when(exists(b - 1))
                def _():
                    await_recv(beside.at[b], trace_recv.at[1, 1 + b])

                total = total + times(beside[b], bands, at, b)
            result[d] = total.astype(BF16)

        @pl.when(jnp.logical_not(computes(d) | is_source(d) | last))
        def _():
            await_recv(result.at[d], hand_recv.at[d])

    out_ref[0] = (result[0].astype(F32) + result[1].astype(F32)).astype(BF16)

    @pl.when(between)
    def _():
        finish()

        @pl.when(late)
        def _():
            forward(1, wait_send)
            hand(1, 1 - early, True).wait_send()


def shards(down_sources, up_sources, down_tiles, up_tiles, tile_rows, tile_cols, shot_order):
    shots, width = down_sources.shape[1:]
    count = down_tiles.shape[1]
    anywhere = pl.BlockSpec(memory_space=pl.ANY)
    dma = pltpu.SemaphoreType.DMA
    return pl.pallas_call(
        kernel,
        name="sweeps",
        out_shape=pltpu.VMEM(down_sources.shape, BF16),
        in_specs=[anywhere] * 7,
        out_specs=pl.BlockSpec(memory_space=pltpu.VMEM),
        scratch_shapes=[
            pltpu.SMEM((count,), jnp.int32),
            pltpu.SMEM((count,), jnp.int32),
            pltpu.SMEM(shot_order.shape, jnp.int32),
            pltpu.VMEM((2, shots, width), BF16),
            pltpu.VMEM((2, count, TILE, TILE), BF16),
            pltpu.VMEM((OUTGOING + 2, 10 * TILE, TILE), BF16),
            pltpu.VMEM((OUTGOING + 2, shots, width), BF16),
            pltpu.VMEM((3, shots, width), BF16),
            pltpu.VMEM((2, shots, width), BF16),
            pltpu.VMEM((2, shots, width), BF16),
            pltpu.VMEM((2, 5, shots, width), BF16),
            pltpu.VMEM((3, shots, width), BF16),
            pltpu.VMEM((5, width, width), BF16),
            pltpu.VMEM((2, shots, width), BF16),
            dma((3,)),
            dma,
            dma,
            dma((4, 2)),
            dma((OUTGOING, 2)),
            dma((3,)),
            dma((2,)),
            dma((2, 5)),
            dma((2,)),
            dma((2,)),
            pltpu.SemaphoreType.REGULAR,
            pltpu.SemaphoreType.REGULAR,
        ],
        compiler_params=pltpu.CompilerParams(collective_id=0, has_side_effects=True),
    )(tile_rows[0], tile_cols[0], shot_order, down_sources, up_sources, down_tiles, up_tiles)


def solution(mesh):
    return jax.shard_map(
        shards,
        mesh=mesh,
        in_specs=(
            P("layer", None, "rows"),
            P("layer", None, "rows"),
            P("layer", "rows", None, None),
            P("layer", "rows", None, None),
            P("layer", "rows"),
            P("layer", "rows"),
            P(),
        ),
        out_specs=P("layer", None, "rows"),
        check_vma=False,
    )
```

```python
import jax
import jax.numpy as jnp
from jax import lax
from jax.experimental import pallas as pl
from jax.experimental.pallas import tpu as pltpu
from jax.sharding import PartitionSpec as P

TILE = 128
MESH = pl.DeviceIdType.MESH
F32 = jnp.float32
BF16 = jnp.bfloat16
LEFT, HOME, RIGHT, SECOND = range(4)
SLOTS = 4
OUTGOING = 2 * SLOTS
PART = 16
PLANE = 4


REACH = 5 * TILE
TERM = 64


def band_rows(c, r):
    return r * REACH + (c - r) * TILE


def band_block(bands, slot, b):
    def tile(c, r):
        return bands[slot, pl.ds(band_rows(c, r), TILE), :]

    def line(r):
        pieces = [
            tile(c, r) if abs(c - 2 - r) <= 2 else jnp.zeros((TILE, TILE), BF16)
            for c in (2 * b, 2 * b + 1)
        ]
        return jnp.concatenate(pieces, axis=1)

    return jnp.concatenate([line(0), line(1)], axis=0)


def times_all(block, matrix):
    return lax.dot_general(
        block, matrix, (((1,), (1,)), ((), ())), preferred_element_type=F32
    )


def times(block, bands, slot, b):
    return times_all(block, band_block(bands, slot, b))


def kernel(
    rows_hbm,
    cols_hbm,
    order_hbm,
    down_src,
    up_src,
    down_tiles,
    up_tiles,
    out_ref,
    rows_ref,
    cols_ref,
    order_ref,
    src,
    tiles,
    bands,
    terms,
    first,
    centre,
    second,
    arrived,
    beside,
    outer,
    sums,
    products,
    result,
    scalar_sem,
    src_sem,
    tile_sem,
    band_send,
    band_recv,
    side_send,
    trace_send,
    trace_recv,
    hand_send,
    hand_recv,
    go,
    far,
):
    devices = lax.axis_size("rows")
    layer, k = lax.axis_index("layer"), lax.axis_index("rows")
    shots, width = src.shape[1], src.shape[2]
    local = width // TILE
    count = tiles.shape[1]
    x, core = layer // 2, layer % 2
    partner = 1 - core
    early = x // 2

    def stage_of(d):
        return x + d * (3 - 2 * x)

    def layer_in(d):
        return core + d * (1 - 2 * core)

    def stage_core(d, at):
        return 1 - d * (at == 0).astype(jnp.int32)

    def event_of(d):
        return stage_of(d) // 2

    def is_source(d):
        return (stage_of(d) == 0) & (layer_in(d) == 0)

    def computes(d):
        return core == stage_core(d, x)

    def own_slot(d):
        inside = event_of(d) * SLOTS + jnp.where(layer_in(d) == 0, HOME, SECOND)
        return jnp.where(computes(d) & jnp.logical_not(is_source(d)), inside, OUTGOING + d)

    scalar_copies = [
        pltpu.make_async_copy(a, b, scalar_sem.at[i])
        for i, (a, b) in enumerate(
            ((rows_hbm, rows_ref), (cols_hbm, cols_ref), (order_hbm, order_ref))
        )
    ]
    src_copies = [
        pltpu.make_async_copy(ref.at[0], src.at[d], src_sem)
        for d, ref in enumerate((down_src, up_src))
    ]
    tile_copies = [
        pltpu.make_async_copy(ref.at[0], tiles.at[d], tile_sem)
        for d, ref in enumerate((down_tiles, up_tiles))
    ]

    def exists(s):
        return (k + s >= 0) & (k + s < devices)

    def present(s):
        return exists(s).astype(jnp.int32)

    barrier = pltpu.get_barrier_semaphore()

    def greet(condition, x_to, core_to, s):
        @pl.when(condition & exists(s))
        def _():
            pl.semaphore_signal(
                barrier, inc=1, device_id=(x_to * 2 + core_to, k + s), device_id_type=MESH
            )

    on_one = core == 1
    for s in (-1, 1):
        greet(on_one | (x == 0), x, partner, s)
        greet(on_one & (x >= 1), x, core, s)
    greet(True, x, partner, 0)
    for copy in scalar_copies + src_copies + tile_copies:
        copy.start()
    def collector(x_to):
        return (x_to <= 1).astype(jnp.int32)

    for s in (-2, 2, -1, 1, 0):
        greet(on_one & (x >= 1), x - 1, collector(x - 1), s)
        onto = (on_one & (x >= 1) & (x <= 2)) | (jnp.logical_not(on_one) & (x == 0))
        greet(onto, x + 1, collector(x + 1), s)
    tail = jnp.where(x == 0, on_one, jnp.logical_not(on_one) & (x == 3))
    for s in (-1, 1, 0):
        to = jnp.where(x == 0, x + 1, x - 1)
        greet(tail, to, collector(to), s)

    for e in range(2):
        for s in (-2, -1, 1, 2):

            @pl.when(jnp.logical_not(exists(s)))
            def _():
                arrived[e, 2 + s] = jnp.zeros_like(arrived[e, 2 + s])

        for s in (-1, 1):

            @pl.when(jnp.logical_not(exists(s)))
            def _():
                at = e * SLOTS + 1 + s
                if e == 0:
                    first[1 + s] = jnp.zeros_like(first[1 + s])
                    beside[1 + s] = jnp.zeros_like(beside[1 + s])
                terms[at] = jnp.zeros_like(terms[at])
                bands[at] = jnp.zeros_like(bands[at])

    for copy in scalar_copies:
        copy.wait()
    slot_of = lax.broadcasted_iota(jnp.int32, (shots, shots), 0)
    shot_of = lax.broadcasted_iota(jnp.int32, (shots, shots), 1)
    wanted = jnp.zeros((shots, shots), jnp.int32)
    for j in range(shots):
        wanted = jnp.where(slot_of == j, order_ref[j], wanted)
    pick = (shot_of == wanted).astype(F32).astype(BF16)
    pltpu.make_async_copy(src, src, src_sem).wait()
    for d in range(2):
        term = jnp.dot(pick, src[d], preferred_element_type=F32).astype(BF16)
        terms[own_slot(d)] = term

        @pl.when(is_source(d))
        def _():
            result[d] = term
            if d == 1:
                first[HOME] = term

    place = []
    for t in range(count):
        row = rows_ref[t] - k * local
        col = cols_ref[t] - (k - 1) * local
        place.append(row * 3 * local + col)

    steps = TILE // PART
    early_slot = jnp.where(early == 0, own_slot(0), own_slot(1))
    late_slot = jnp.where(early == 0, own_slot(1), own_slot(0))

    def build(late, r):
        sweep = (early + late) % 2
        slot = late_slot if late else early_slot

        def step(part, carry):
            lines = pl.ds(pl.multiple_of(part * PART, PART), PART)
            pieces = [tiles[sweep, t, lines, :].astype(F32) for t in range(count)]
            for c in range(r, r + 5):
                total = jnp.zeros((PART, TILE), F32)
                for t in range(count):
                    total = total + jnp.where(place[t] == r * 3 * local + c, pieces[t], 0.0)
                at = pl.ds(pl.multiple_of(band_rows(c, r) + part * PART, PART), PART)
                bands[slot, at, :] = total.astype(BF16)
            return carry

        lax.fori_loop(0, steps, step, 0)

    def send(source, target, send_sem, recv_sem, x_to, core_to, s):
        return pltpu.make_async_remote_copy(
            src_ref=source,
            dst_ref=target,
            send_sem=send_sem,
            recv_sem=recv_sem,
            device_id=(x_to * 2 + core_to, k + s),
            device_id_type=MESH,
        )

    def await_recv(buffer, sem):
        pltpu.make_async_remote_copy(
            src_ref=buffer,
            dst_ref=buffer,
            send_sem=hand_send.at[0],
            recv_sem=sem,
            device_id=(layer, k),
            device_id_type=MESH,
        ).wait_recv()

    start = lambda copy: copy.start()
    wait_send = lambda copy: copy.wait_send()

    def leaves_plane(s):
        return (k % PLANE + s) // PLANE != 0

    def give(condition, d, act, seconds, lines=(0, 1), crossing=None):
        for s in (0,) if seconds else (-1, 1, 0):
            remote = exists(s) if s else core != stage_core(d, x)
            kind = layer_in(d) == (1 if seconds else 0)
            if crossing is not None:
                kind = kind & (leaves_plane(s) == crossing)

            @pl.when(condition & remote & kind & jnp.logical_not(is_source(d)))
            def _():
                at = own_slot(d)
                to = event_of(d) * SLOTS + (SECOND if seconds else 1 - s)
                lane = 3 if seconds else 1 + s

                def part(source, target, r):
                    return send(
                        source,
                        target,
                        band_send.at[lane, r],
                        band_recv.at[to, r],
                        x,
                        stage_core(d, x),
                        s,
                    )

                for r in lines:
                    if act is wait_send:
                        both = bands.at[at, pl.ds(0, REACH + r * TERM)]
                        part(both, both, r).wait_send()
                        continue
                    piece = pl.ds(r * REACH, REACH)
                    act(part(bands.at[at, piece], bands.at[to, piece], r))
                    if r == 1:
                        act(part(terms.at[at], terms.at[to], r))

    def sources(d, act):
        for s in (-1, 1, 0):
            remote = exists(s) if s else core != stage_core(d, x)

            @pl.when(is_source(d) & remote)
            def _():
                act(
                    send(
                        terms.at[OUTGOING + d],
                        first.at[1 - s],
                        side_send.at[1 + s],
                        trace_recv.at[0, 2 - s],
                        x,
                        stage_core(d, x),
                        s,
                    )
                )

    def forward(e, act):
        d = (early + e) % 2
        to = x + 1 - 2 * d
        slot = (stage_of(d) + 1) // 2

        def main(s):
            return send(
                second.at[e],
                arrived.at[slot, 2 - s],
                trace_send.at[e],
                trace_recv.at[slot, 2 - s],
                to,
                stage_core(d, to),
                s,
            )

        def extra(s):
            return send(
                second.at[e],
                beside.at[1 - s],
                side_send.at[1 + s],
                trace_recv.at[1, 2 - s],
                to,
                1 - stage_core(d, to),
                s,
            )

        if act is wait_send:
            for n in (3, 4, 5):

                @pl.when(spread == n)
                def _():
                    blocks = arrived.at[0, pl.ds(0, n)]
                    send(blocks, blocks, trace_send.at[e], trace_recv.at[0, 0], x, partner, 0).wait_send()

            if e == 1:
                for s in (-1, 1, 0):

                    @pl.when(exists(s))
                    def _():
                        extra(s).wait_send()

            return

        for crossing in (True, False):
            for copies, reached in ((main, (-1, 1, -2, 2, 0)), (extra, (-1, 1, 0))):
                if copies is extra and e == 0:
                    continue
                for s in reached:
                    if crossing and s == 0:
                        continue
                    side = leaves_plane(s)

                    @pl.when(exists(s) & (side if crossing else jnp.logical_not(side)))
                    def _():
                        act(copies(s))

    def hand(e, d, from_second):
        return send(
            second.at[e] if from_second else centre.at[e],
            result.at[d],
            hand_send.at[e],
            hand_recv.at[d],
            x,
            partner,
            0,
        )

    origin = is_source(0) | is_source(1)

    pltpu.make_async_copy(tiles, tiles, tile_sem).wait()

    @pl.when(jnp.logical_not(origin))
    def _():
        build(0, 0)

    patient = jnp.logical_not(on_one) & (x >= 2)

    @pl.when(patient)
    def _():
        build(0, 1)

    reach = present(-1) + present(0) + present(1)
    spread = reach + present(-2) + present(2)
    onward = (x <= 2).astype(jnp.int32) + (x >= 1).astype(jnp.int32)
    between = (x >= 1) & (x <= 2)
    collects = core == collector(x)
    pl.semaphore_wait(
        barrier,
        reach
        + collects.astype(jnp.int32) * (onward * spread + between.astype(jnp.int32) * reach),
    )

    @pl.when(collects & (x >= 2))
    def _():
        pl.semaphore_signal(far, inc=1, device_id=(x * 2 + partner, k), device_id_type=MESH)

    for d in range(2):
        sources(d, start)
    for d in range(2):
        for seconds in (False, True):
            give(event_of(d) == 0, d, start, seconds, (0,))

    @pl.when(jnp.logical_not(origin | patient))
    def _():
        build(0, 1)

    for d in range(2):
        for seconds in (False, True):
            give(event_of(d) == 0, d, start, seconds, (1,))
    for r in range(2):
        build(1, r)
    for d in range(2):
        give(event_of(d) == 1, d, start, True)

    def let_go():
        pl.semaphore_signal(go, inc=1, device_id=(x * 2 + partner, k), device_id_type=MESH)

    leads = between & (core == early)
    follows = between & (core != early)
    for d in range(2):
        give(leads & (event_of(d) == 0), d, wait_send, False, (0,))

    @pl.when(leads)
    def _():
        let_go()

    @pl.when(follows)
    def _():
        pl.semaphore_wait(go, 1)

    for d in range(2):
        give(follows & (event_of(d) == 1), d, start, False)

    def event(e):
        d = (early + e) % 2
        X = stage_of(d)
        base = e * SLOTS
        ends_second = (d == 0) | (x == 0)

        def await_band(slot):
            here = exists(slot - 1)
            if slot is HOME:
                here = ends_second
            if slot is SECOND:
                here = jnp.logical_not(ends_second)

            @pl.when(here)
            def _():
                for r in range(2):
                    piece = bands.at[base + slot, pl.ds(0, REACH + r * TERM)]
                    await_recv(piece, band_recv.at[base + slot, r])

        if e == 0:

            @pl.when(X == 0)
            def _():
                await_band(SECOND)
                total = terms[base + SECOND].astype(F32)
                for b in (1, 0, 2):

                    @pl.when(exists(b - 1) if b != 1 else d == 0)
                    def _():
                        await_recv(first.at[b], trace_recv.at[0, 1 + b])

                    total = total + times(first[b], bands, base + SECOND, b)
                second[e] = total.astype(BF16)

        def await_block(block):
            @pl.when((k + block - 2 >= 0) & (k + block - 2 < devices))
            def _():
                await_recv(arrived.at[e, block], trace_recv.at[e, block])

        @pl.when(X >= 1)
        def _():
            turn = 1 - 2 * (k % PLANE >= PLANE // 2).astype(jnp.int32)
            await_band(SECOND)
            for t in range(3):
                outer[t] = band_block(bands, base + SECOND, t)
            for block in (0, 4):
                sums[block] = jnp.zeros_like(sums[block])
            total = terms[base + SECOND].astype(F32)
            for t in (HOME, 1 + turn, 1 - turn):
                await_band(t)
                total = total + times_all(terms[base + t], outer[t])
                for b in range(3):
                    product = jnp.dot(
                        outer[t], band_block(bands, base + t, b), preferred_element_type=F32
                    )
                    sums[t + b] = product if t is HOME else sums[t + b] + product
            for block in range(5):
                products[block] = sums[block].astype(BF16)
            for j in (0, 1, 2, -1, -2):
                block = 2 + j * turn
                await_block(block)
                total = total + times_all(arrived[e, block], products[block])
            second[e] = total.astype(BF16)

        if e == 0:

            @pl.when(x >= 2)
            def _():
                pl.semaphore_wait(far, 1)

        @pl.when(X < 3)
        def _():
            forward(e, start)

        @pl.when((X == 1) | (X == 2))
        def _():
            inner = terms[base + HOME].astype(F32)
            for b in range(3):
                inner = inner + times(arrived[e, 1 + b], bands, base + HOME, b)
            centre[e] = inner.astype(BF16)

            @pl.when(ends_second)
            def _():
                hand(e, d, False).start()

        @pl.when(ends_second)
        def _():
            result[d] = second[e]

        @pl.when(jnp.logical_not(ends_second))
        def _():
            hand(e, d, True).start()

            @pl.when(X >= 1)
            def _():
                result[d] = centre[e]

    @pl.when(on_one)
    def _():
        event(0)

    @pl.when(on_one & (x == 3))
    def _():
        let_go()

    @pl.when(jnp.logical_not(on_one) & (x == 3))
    def _():
        pl.semaphore_wait(go, 1)

    for d in range(2):
        give(((x == 0) | (x == 3)) & (event_of(d) == 1), d, start, False)

    late = on_one != (x == 0)

    def finish():
        for d in range(2):
            sources(d, wait_send)
            led = leads & (event_of(d) == 0)
            give(led, d, wait_send, False, (1,))
            give(jnp.logical_not(led), d, wait_send, False)
            give(True, d, wait_send, True)

        @pl.when(on_one)
        def _():
            forward(0, wait_send)

            @pl.when(x != 0)
            def _():
                hand(0, early, True).wait_send()

    @pl.when(jnp.logical_not(between))
    def _():
        finish()

    @pl.when(late)
    def _():
        event(1)

    for d in range(2):
        last = stage_of(d) == 3

        @pl.when(tail & last)
        def _():
            at = OUTGOING + d
            total = terms[at].astype(F32)
            for b in (1, 0, 2):

                @pl.when(exists(b - 1))
                def _():
                    await_recv(beside.at[b], trace_recv.at[1, 1 + b])

                total = total + times(beside[b], bands, at, b)
            result[d] = total.astype(BF16)

        @pl.when(jnp.logical_not(computes(d) | is_source(d) | last))
        def _():
            await_recv(result.at[d], hand_recv.at[d])

    out_ref[0] = (result[0].astype(F32) + result[1].astype(F32)).astype(BF16)

    @pl.when(between)
    def _():
        finish()

        @pl.when(late)
        def _():
            forward(1, wait_send)
            hand(1, 1 - early, True).wait_send()


def shards(down_sources, up_sources, down_tiles, up_tiles, tile_rows, tile_cols, shot_order):
    shots, width = down_sources.shape[1:]
    count = down_tiles.shape[1]
    anywhere = pl.BlockSpec(memory_space=pl.ANY)
    dma = pltpu.SemaphoreType.DMA
    return pl.pallas_call(
        kernel,
        name="sweeps",
        out_shape=pltpu.VMEM(down_sources.shape, BF16),
        in_specs=[anywhere] * 7,
        out_specs=pl.BlockSpec(memory_space=pltpu.VMEM),
        scratch_shapes=[
            pltpu.SMEM((count,), jnp.int32),
            pltpu.SMEM((count,), jnp.int32),
            pltpu.SMEM(shot_order.shape, jnp.int32),
            pltpu.VMEM((2, shots, width), BF16),
            pltpu.VMEM((2, count, TILE, TILE), BF16),
            pltpu.VMEM((OUTGOING + 2, 10 * TILE, TILE), BF16),
            pltpu.VMEM((OUTGOING + 2, shots, width), BF16),
            pltpu.VMEM((3, shots, width), BF16),
            pltpu.VMEM((2, shots, width), BF16),
            pltpu.VMEM((2, shots, width), BF16),
            pltpu.VMEM((2, 5, shots, width), BF16),
            pltpu.VMEM((3, shots, width), BF16),
            pltpu.VMEM((3, width, width), BF16),
            pltpu.VMEM((5, width, width), F32),
            pltpu.VMEM((5, width, width), BF16),
            pltpu.VMEM((2, shots, width), BF16),
            dma((3,)),
            dma,
            dma,
            dma((4, 2)),
            dma((OUTGOING, 2)),
            dma((3,)),
            dma((2,)),
            dma((2, 5)),
            dma((2,)),
            dma((2,)),
            pltpu.SemaphoreType.REGULAR,
            pltpu.SemaphoreType.REGULAR,
        ],
        compiler_params=pltpu.CompilerParams(collective_id=0, has_side_effects=True),
    )(tile_rows[0], tile_cols[0], shot_order, down_sources, up_sources, down_tiles, up_tiles)


def solution(mesh):
    return jax.shard_map(
        shards,
        mesh=mesh,
        in_specs=(
            P("layer", None, "rows"),
            P("layer", None, "rows"),
            P("layer", "rows", None, None),
            P("layer", "rows", None, None),
            P("layer", "rows"),
            P("layer", "rows"),
            P(),
        ),
        out_specs=P("layer", None, "rows"),
        check_vma=False,
    )
```

```python
import jax
import jax.numpy as jnp
from jax import lax
from jax.experimental import pallas as pl
from jax.experimental.pallas import tpu as pltpu
from jax.sharding import PartitionSpec as P

TILE = 128
MESH = pl.DeviceIdType.MESH
F32 = jnp.float32
BF16 = jnp.bfloat16
LEFT, HOME, RIGHT, SECOND = range(4)
SLOTS = 4
OUTGOING = 2 * SLOTS
PART = 16
PLANE = 4


REACH = 5 * TILE
TERM = 64


def band_rows(c, r):
    return r * REACH + (c - r) * TILE


def band_block(bands, slot, b):
    def tile(c, r):
        return bands[slot, pl.ds(band_rows(c, r), TILE), :]

    def line(r):
        pieces = [
            tile(c, r) if abs(c - 2 - r) <= 2 else jnp.zeros((TILE, TILE), BF16)
            for c in (2 * b, 2 * b + 1)
        ]
        return jnp.concatenate(pieces, axis=1)

    return jnp.concatenate([line(0), line(1)], axis=0)


def times_all(block, matrix):
    return lax.dot_general(
        block, matrix, (((1,), (1,)), ((), ())), preferred_element_type=F32
    )


def times(block, bands, slot, b):
    return times_all(block, band_block(bands, slot, b))


def kernel(
    rows_hbm,
    cols_hbm,
    order_hbm,
    down_src,
    up_src,
    down_tiles,
    up_tiles,
    out_ref,
    rows_ref,
    cols_ref,
    order_ref,
    src,
    tiles,
    bands,
    terms,
    first,
    centre,
    second,
    arrived,
    beside,
    outer,
    sums,
    products,
    result,
    scalar_sem,
    src_sem,
    tile_sem,
    band_send,
    band_recv,
    side_send,
    trace_send,
    trace_recv,
    hand_send,
    hand_recv,
    go,
):
    devices = lax.axis_size("rows")
    layer, k = lax.axis_index("layer"), lax.axis_index("rows")
    shots, width = src.shape[1], src.shape[2]
    local = width // TILE
    count = tiles.shape[1]
    x, core = layer // 2, layer % 2
    partner = 1 - core
    early = x // 2

    def stage_of(d):
        return x + d * (3 - 2 * x)

    def layer_in(d):
        return core + d * (1 - 2 * core)

    def stage_core(d, at):
        return 1 - d * (at == 0).astype(jnp.int32)

    def event_of(d):
        return stage_of(d) // 2

    def is_source(d):
        return (stage_of(d) == 0) & (layer_in(d) == 0)

    def computes(d):
        return core == stage_core(d, x)

    def own_slot(d):
        inside = event_of(d) * SLOTS + jnp.where(layer_in(d) == 0, HOME, SECOND)
        return jnp.where(computes(d) & jnp.logical_not(is_source(d)), inside, OUTGOING + d)

    scalar_copies = [
        pltpu.make_async_copy(a, b, scalar_sem.at[i])
        for i, (a, b) in enumerate(
            ((rows_hbm, rows_ref), (cols_hbm, cols_ref), (order_hbm, order_ref))
        )
    ]
    src_copies = [
        pltpu.make_async_copy(ref.at[0], src.at[d], src_sem)
        for d, ref in enumerate((down_src, up_src))
    ]
    tile_copies = [
        pltpu.make_async_copy(ref.at[0], tiles.at[d], tile_sem)
        for d, ref in enumerate((down_tiles, up_tiles))
    ]

    def exists(s):
        return (k + s >= 0) & (k + s < devices)

    def present(s):
        return exists(s).astype(jnp.int32)

    barrier = pltpu.get_barrier_semaphore()

    def greet(condition, x_to, core_to, s):
        @pl.when(condition & exists(s))
        def _():
            pl.semaphore_signal(
                barrier, inc=1, device_id=(x_to * 2 + core_to, k + s), device_id_type=MESH
            )

    on_one = core == 1
    for s in (-1, 1):
        greet(on_one | (x == 0), x, partner, s)
        greet(on_one & (x >= 1), x, core, s)
    greet(True, x, partner, 0)
    for copy in scalar_copies + src_copies + tile_copies:
        copy.start()
    def collector(x_to):
        return (x_to <= 1).astype(jnp.int32)

    for s in (-2, 2, -1, 1, 0):
        greet(on_one & (x >= 1), x - 1, collector(x - 1), s)
        onto = (on_one & (x >= 1) & (x <= 2)) | (jnp.logical_not(on_one) & (x == 0))
        greet(onto, x + 1, collector(x + 1), s)
    tail = jnp.where(x == 0, on_one, jnp.logical_not(on_one) & (x == 3))
    for s in (-1, 1, 0):
        to = jnp.where(x == 0, x + 1, x - 1)
        greet(tail, to, collector(to), s)

    for e in range(2):
        for s in (-2, -1, 1, 2):

            @pl.when(jnp.logical_not(exists(s)))
            def _():
                arrived[e, 2 + s] = jnp.zeros_like(arrived[e, 2 + s])

        for s in (-1, 1):

            @pl.when(jnp.logical_not(exists(s)))
            def _():
                at = e * SLOTS + 1 + s
                if e == 0:
                    first[1 + s] = jnp.zeros_like(first[1 + s])
                    beside[1 + s] = jnp.zeros_like(beside[1 + s])
                terms[at] = jnp.zeros_like(terms[at])
                bands[at] = jnp.zeros_like(bands[at])

    for copy in scalar_copies:
        copy.wait()
    slot_of = lax.broadcasted_iota(jnp.int32, (shots, shots), 0)
    shot_of = lax.broadcasted_iota(jnp.int32, (shots, shots), 1)
    wanted = jnp.zeros((shots, shots), jnp.int32)
    for j in range(shots):
        wanted = jnp.where(slot_of == j, order_ref[j], wanted)
    pick = (shot_of == wanted).astype(F32).astype(BF16)
    pltpu.make_async_copy(src, src, src_sem).wait()
    for d in range(2):
        term = jnp.dot(pick, src[d], preferred_element_type=F32).astype(BF16)
        terms[own_slot(d)] = term

        @pl.when(is_source(d))
        def _():
            result[d] = term
            if d == 1:
                first[HOME] = term

    place = []
    for t in range(count):
        row = rows_ref[t] - k * local
        col = cols_ref[t] - (k - 1) * local
        place.append(row * 3 * local + col)

    steps = TILE // PART
    early_slot = jnp.where(early == 0, own_slot(0), own_slot(1))
    late_slot = jnp.where(early == 0, own_slot(1), own_slot(0))

    def build(late, r):
        sweep = (early + late) % 2
        slot = late_slot if late else early_slot

        def step(part, carry):
            lines = pl.ds(pl.multiple_of(part * PART, PART), PART)
            pieces = [tiles[sweep, t, lines, :].astype(F32) for t in range(count)]
            for c in range(r, r + 5):
                total = jnp.zeros((PART, TILE), F32)
                for t in range(count):
                    total = total + jnp.where(place[t] == r * 3 * local + c, pieces[t], 0.0)
                at = pl.ds(pl.multiple_of(band_rows(c, r) + part * PART, PART), PART)
                bands[slot, at, :] = total.astype(BF16)
            return carry

        lax.fori_loop(0, steps, step, 0)

    def send(source, target, send_sem, recv_sem, x_to, core_to, s):
        return pltpu.make_async_remote_copy(
            src_ref=source,
            dst_ref=target,
            send_sem=send_sem,
            recv_sem=recv_sem,
            device_id=(x_to * 2 + core_to, k + s),
            device_id_type=MESH,
        )

    def await_recv(buffer, sem):
        pltpu.make_async_remote_copy(
            src_ref=buffer,
            dst_ref=buffer,
            send_sem=hand_send,
            recv_sem=sem,
            device_id=(layer, k),
            device_id_type=MESH,
        ).wait_recv()

    turn = 1 - 2 * (k % PLANE >= PLANE // 2).astype(jnp.int32)

    def leaves_plane(s):
        return (k % PLANE + s) // PLANE != 0

    def give(condition, d, seconds, lines=(0, 1)):
        for s in (0,) if seconds else (-1, 1, 0):
            remote = exists(s) if s else core != stage_core(d, x)
            kind = layer_in(d) == (1 if seconds else 0)

            @pl.when(condition & remote & kind & jnp.logical_not(is_source(d)))
            def _():
                at = own_slot(d)
                to = event_of(d) * SLOTS + (SECOND if seconds else 1 - s)

                def part(source, target, r):
                    return send(
                        source,
                        target,
                        band_send.at[2 if seconds else r],
                        band_recv.at[to],
                        x,
                        stage_core(d, x),
                        s,
                    )

                for r in lines:
                    piece = pl.ds(r * REACH, REACH)
                    part(bands.at[at, piece], bands.at[to, piece], r).start()
                    if r == 1:
                        part(terms.at[at], terms.at[to], r).start()

    def await_sent(condition, buffer, sem):
        @pl.when(condition)
        def _():
            send(buffer, buffer, sem, band_recv.at[0], x, partner, 0).wait_send()

    def await_given(condition, d, lines):
        targets = present(-1) + present(1) + (core != stage_core(d, x)).astype(jnp.int32)
        ours = condition & (layer_in(d) == 0) & jnp.logical_not(is_source(d))
        for n in (1, 2, 3):
            for r in lines:
                size = bands.at[pl.ds(0, n), pl.ds(0, REACH + r * TERM)]
                await_sent(ours & (targets == n), size, band_send.at[r])

    whole = bands.at[pl.ds(0, 2), pl.ds(0, REACH + TERM // 2)]

    def await_seconds(d):
        remote = core != stage_core(d, x)
        await_sent(remote & (layer_in(d) == 1), whole, band_send.at[2])

    def blocks(n):
        return arrived.at[0, pl.ds(0, n)]

    def sources(d):
        for s in (-1, 1, 0):
            remote = exists(s) if s else core != stage_core(d, x)

            @pl.when(is_source(d) & remote)
            def _():
                send(
                    terms.at[OUTGOING + d],
                    first.at[1 - s],
                    side_send,
                    trace_recv.at[0, 2 - s],
                    x,
                    stage_core(d, x),
                    s,
                ).start()

    def await_sources(d):
        targets = present(-1) + present(1) + (core != stage_core(d, x)).astype(jnp.int32)
        for n in (1, 2, 3):
            await_sent(is_source(d) & (targets == n), blocks(n), side_send)

    def await_forward(e):
        for n in (3, 4, 5):
            await_sent(spread == n, blocks(n), trace_send.at[e])
        if e == 1:
            for n in (2, 3):
                await_sent(reach == n, blocks(n), side_send)

    def forward(e):
        d = (early + e) % 2
        to = x + 1 - 2 * d
        slot = (stage_of(d) + 1) // 2

        def main(s):
            return send(
                second.at[e],
                arrived.at[slot, 2 - s],
                trace_send.at[e],
                trace_recv.at[slot, 2 - s],
                to,
                stage_core(d, to),
                s,
            )

        def extra(s):
            return send(
                second.at[e],
                beside.at[1 - s],
                side_send,
                trace_recv.at[1, 2 - s],
                to,
                1 - stage_core(d, to),
                s,
            )

        for crossing in (True, False):
            for copies, reached in ((main, (-1, 1)), (extra, (-1, 1)), (main, (-2, 2, 0)), (extra, (0,))):
                if copies is extra and e == 0:
                    continue
                for s in reached:
                    if crossing and s == 0:
                        continue
                    side = leaves_plane(s)

                    @pl.when(exists(s) & (side if crossing else jnp.logical_not(side)))
                    def _():
                        copies(s).start()

    def hand(e, d, from_second):
        return send(
            second.at[e] if from_second else centre.at[e],
            result.at[d],
            hand_send,
            hand_recv.at[d],
            x,
            partner,
            0,
        )

    origin = is_source(0) | is_source(1)

    pltpu.make_async_copy(tiles, tiles, tile_sem).wait()

    @pl.when(jnp.logical_not(origin))
    def _():
        build(0, 0)

    patient = jnp.logical_not(on_one) & (x >= 2)

    @pl.when(patient)
    def _():
        build(0, 1)

    reach = present(-1) + present(0) + present(1)
    spread = reach + present(-2) + present(2)
    onward = (x <= 2).astype(jnp.int32) + (x >= 1).astype(jnp.int32)
    between = (x >= 1) & (x <= 2)
    collects = core == collector(x)
    pl.semaphore_wait(
        barrier,
        reach
        + collects.astype(jnp.int32) * (onward * spread + between.astype(jnp.int32) * reach),
    )

    @pl.when(collects & (x >= 2))
    def _():
        pl.semaphore_signal(go, inc=1, device_id=(x * 2 + partner, k), device_id_type=MESH)

    for d in range(2):
        sources(d)
    for d in range(2):
        for seconds in (False, True):
            give(event_of(d) == 0, d, seconds, (0,))

    @pl.when(jnp.logical_not(origin | patient))
    def _():
        build(0, 1)

    for d in range(2):
        for seconds in (False, True):
            give(event_of(d) == 0, d, seconds, (1,))
    for r in range(2):
        build(1, r)
    for d in range(2):
        give(event_of(d) == 1, d, True)

    def let_go():
        pl.semaphore_signal(go, inc=1, device_id=(x * 2 + partner, k), device_id_type=MESH)

    leads = between & (core == early)
    follows = between & (core != early)
    for d in range(2):
        await_given(leads & (event_of(d) == 0), d, (0,))

    @pl.when(leads)
    def _():
        let_go()

    @pl.when(follows)
    def _():
        pl.semaphore_wait(go, 1)

    for d in range(2):
        give(follows & (event_of(d) == 1), d, False)

    def event(e):
        d = (early + e) % 2
        X = stage_of(d)
        base = e * SLOTS
        ends_second = (d == 0) | (x == 0)

        def await_band(slot):
            here = exists(slot - 1)
            if slot is HOME:
                here = ends_second
            if slot is SECOND:
                here = jnp.logical_not(ends_second)

            @pl.when(here)
            def _():
                await_recv(whole, band_recv.at[base + slot])

        if e == 0:

            @pl.when(X == 0)
            def _():
                await_band(SECOND)
                total = terms[base + SECOND].astype(F32)
                for b in (1, 0, 2):

                    @pl.when(exists(b - 1) if b != 1 else d == 0)
                    def _():
                        await_recv(first.at[b], trace_recv.at[0, 1 + b])

                    total = total + times(first[b], bands, base + SECOND, b)
                second[e] = total.astype(BF16)

        def await_block(block):
            @pl.when((k + block - 2 >= 0) & (k + block - 2 < devices))
            def _():
                await_recv(arrived.at[e, block], trace_recv.at[e, block])

        @pl.when(X >= 1)
        def _():
            await_band(SECOND)
            for t in range(3):
                outer[t] = band_block(bands, base + SECOND, t)
            for block in (0, 4):
                sums[block] = jnp.zeros_like(sums[block])
            total = terms[base + SECOND].astype(F32)
            for t in (HOME, 1 + turn, 1 - turn):
                await_band(t)
                total = total + times_all(terms[base + t], outer[t])
                for b in range(3):
                    product = jnp.dot(
                        outer[t], band_block(bands, base + t, b), preferred_element_type=F32
                    )
                    sums[t + b] = product if t is HOME else sums[t + b] + product
            for block in range(5):
                products[block] = sums[block].astype(BF16)
            for j in (0, 1, 2, -1, -2):
                block = 2 + j * turn
                await_block(block)
                total = total + times_all(arrived[e, block], products[block])
            second[e] = total.astype(BF16)

        if e == 0:

            @pl.when(x >= 2)
            def _():
                pl.semaphore_wait(go, 1)

        @pl.when(X < 3)
        def _():
            forward(e)

        @pl.when((X == 1) | (X == 2))
        def _():
            inner = terms[base + HOME].astype(F32)
            for b in range(3):
                inner = inner + times(arrived[e, 1 + b], bands, base + HOME, b)
            centre[e] = inner.astype(BF16)

            @pl.when(ends_second)
            def _():
                hand(e, d, False).start()

        @pl.when(ends_second)
        def _():
            result[d] = second[e]

        @pl.when(jnp.logical_not(ends_second))
        def _():
            hand(e, d, True).start()

            @pl.when(X >= 1)
            def _():
                result[d] = centre[e]

    @pl.when(on_one)
    def _():
        event(0)

    @pl.when(on_one & (x == 3))
    def _():
        let_go()

    @pl.when(jnp.logical_not(on_one) & (x == 3))
    def _():
        pl.semaphore_wait(go, 1)

    for d in range(2):
        give(((x == 0) | (x == 3)) & (event_of(d) == 1), d, False)

    late = on_one != (x == 0)

    def finish():
        for d in range(2):
            await_sources(d)
            led = leads & (event_of(d) == 0)
            await_given(led, d, (1,))
            await_given(jnp.logical_not(led), d, (0, 1))
            await_seconds(d)

        @pl.when(on_one)
        def _():
            await_forward(0)

        await_sent(on_one & (x == 3), blocks(1), hand_send)

    @pl.when(jnp.logical_not(between))
    def _():
        finish()

    @pl.when(late)
    def _():
        event(1)

    for d in range(2):
        last = stage_of(d) == 3

        @pl.when(tail & last)
        def _():
            at = OUTGOING + d
            total = terms[at].astype(F32)
            for b in range(3):
                outer[b] = band_block(bands, at, b)
            for b in (HOME, 1 + turn, 1 - turn):

                @pl.when((k + b - 1 >= 0) & (k + b - 1 < devices))
                def _():
                    await_recv(beside.at[b], trace_recv.at[1, 1 + b])

                total = total + times_all(beside[b], outer[b])
            result[d] = total.astype(BF16)

        @pl.when(jnp.logical_not(computes(d) | is_source(d) | last))
        def _():
            await_recv(result.at[d], hand_recv.at[d])

    out_ref[0] = (result[0].astype(F32) + result[1].astype(F32)).astype(BF16)

    @pl.when(between)
    def _():
        finish()

        @pl.when(late)
        def _():
            await_forward(1)
            await_sent(True, blocks(2), hand_send)


def shards(down_sources, up_sources, down_tiles, up_tiles, tile_rows, tile_cols, shot_order):
    shots, width = down_sources.shape[1:]
    count = down_tiles.shape[1]
    anywhere = pl.BlockSpec(memory_space=pl.ANY)
    dma = pltpu.SemaphoreType.DMA
    return pl.pallas_call(
        kernel,
        name="sweeps",
        out_shape=pltpu.VMEM(down_sources.shape, BF16),
        in_specs=[anywhere] * 7,
        out_specs=pl.BlockSpec(memory_space=pltpu.VMEM),
        scratch_shapes=[
            pltpu.SMEM((count,), jnp.int32),
            pltpu.SMEM((count,), jnp.int32),
            pltpu.SMEM(shot_order.shape, jnp.int32),
            pltpu.VMEM((2, shots, width), BF16),
            pltpu.VMEM((2, count, TILE, TILE), BF16),
            pltpu.VMEM((OUTGOING + 2, 10 * TILE, TILE), BF16),
            pltpu.VMEM((OUTGOING + 2, shots, width), BF16),
            pltpu.VMEM((3, shots, width), BF16),
            pltpu.VMEM((2, shots, width), BF16),
            pltpu.VMEM((2, shots, width), BF16),
            pltpu.VMEM((2, 5, shots, width), BF16),
            pltpu.VMEM((3, shots, width), BF16),
            pltpu.VMEM((3, width, width), BF16),
            pltpu.VMEM((5, width, width), F32),
            pltpu.VMEM((5, width, width), BF16),
            pltpu.VMEM((2, shots, width), BF16),
            dma((3,)),
            dma,
            dma,
            dma((3,)),
            dma((OUTGOING,)),
            dma,
            dma((2,)),
            dma((2, 5)),
            dma,
            dma((2,)),
            pltpu.SemaphoreType.REGULAR,
        ],
        compiler_params=pltpu.CompilerParams(collective_id=0, has_side_effects=True),
    )(tile_rows[0], tile_cols[0], shot_order, down_sources, up_sources, down_tiles, up_tiles)


def solution(mesh):
    return jax.shard_map(
        shards,
        mesh=mesh,
        in_specs=(
            P("layer", None, "rows"),
            P("layer", None, "rows"),
            P("layer", "rows", None, None),
            P("layer", "rows", None, None),
            P("layer", "rows"),
            P("layer", "rows"),
            P(),
        ),
        out_specs=P("layer", None, "rows"),
        check_vma=False,
    )
```

```python
import jax
import jax.numpy as jnp
from jax import lax
from jax.experimental import pallas as pl
from jax.experimental.pallas import tpu as pltpu
from jax.sharding import PartitionSpec as P

TILE = 128
MESH = pl.DeviceIdType.MESH
F32 = jnp.float32
BF16 = jnp.bfloat16
LEFT, HOME, RIGHT, SECOND = range(4)
SLOTS = 4
OUTGOING = 2 * SLOTS
PART = 16
PLANE = 4


REACH = 5 * TILE
TERM = 64


def band_rows(c, r):
    return r * REACH + (c - r) * TILE


def band_block(bands, slot, b):
    def tile(c, r):
        return bands[slot, pl.ds(band_rows(c, r), TILE), :]

    def line(r):
        pieces = [
            tile(c, r) if abs(c - 2 - r) <= 2 else jnp.zeros((TILE, TILE), BF16)
            for c in (2 * b, 2 * b + 1)
        ]
        return jnp.concatenate(pieces, axis=1)

    return jnp.concatenate([line(0), line(1)], axis=0)


def times_all(block, matrix):
    return lax.dot_general(
        block, matrix, (((1,), (1,)), ((), ())), preferred_element_type=F32
    )


def times(block, bands, slot, b):
    return times_all(block, band_block(bands, slot, b))


def kernel(
    rows_hbm,
    cols_hbm,
    order_hbm,
    down_src,
    up_src,
    down_tiles,
    up_tiles,
    out_ref,
    rows_ref,
    cols_ref,
    order_ref,
    src,
    tiles,
    bands,
    terms,
    first,
    centre,
    second,
    arrived,
    beside,
    outer,
    sums,
    products,
    result,
    scalar_sem,
    src_sem,
    tile_sem,
    band_send,
    band_recv,
    side_send,
    trace_send,
    trace_recv,
    hand_send,
    hand_recv,
    go,
):
    devices = lax.axis_size("rows")
    layer, k = lax.axis_index("layer"), lax.axis_index("rows")
    shots, width = src.shape[1], src.shape[2]
    local = width // TILE
    count = tiles.shape[1]
    x, core = layer // 2, layer % 2
    partner = 1 - core
    early = x // 2

    def stage_of(d):
        return x + d * (3 - 2 * x)

    def layer_in(d):
        return core + d * (1 - 2 * core)

    def stage_core(d, at):
        return 1 - d * (at == 0).astype(jnp.int32)

    def event_of(d):
        return stage_of(d) // 2

    def is_source(d):
        return (stage_of(d) == 0) & (layer_in(d) == 0)

    def computes(d):
        return core == stage_core(d, x)

    def own_slot(d):
        inside = event_of(d) * SLOTS + jnp.where(layer_in(d) == 0, HOME, SECOND)
        return jnp.where(computes(d) & jnp.logical_not(is_source(d)), inside, OUTGOING + d)

    scalar_copies = [
        pltpu.make_async_copy(a, b, scalar_sem.at[i])
        for i, (a, b) in enumerate(
            ((rows_hbm, rows_ref), (cols_hbm, cols_ref), (order_hbm, order_ref))
        )
    ]
    src_copies = [
        pltpu.make_async_copy(ref.at[0], src.at[d], src_sem)
        for d, ref in enumerate((down_src, up_src))
    ]
    tile_copies = [
        pltpu.make_async_copy(ref.at[0], tiles.at[d], tile_sem)
        for d, ref in enumerate((down_tiles, up_tiles))
    ]

    def exists(s):
        return (k + s >= 0) & (k + s < devices)

    def present(s):
        return exists(s).astype(jnp.int32)

    barrier = pltpu.get_barrier_semaphore()

    def greet(condition, x_to, core_to, s):
        @pl.when(condition & exists(s))
        def _():
            pl.semaphore_signal(
                barrier, inc=1, device_id=(x_to * 2 + core_to, k + s), device_id_type=MESH
            )

    on_one = core == 1
    for s in (-1, 1):
        greet(on_one | (x == 0), x, partner, s)
        greet(on_one & (x >= 1), x, core, s)
    greet(True, x, partner, 0)
    for copy in scalar_copies + src_copies + tile_copies:
        copy.start()
    def collector(x_to):
        return (x_to <= 1).astype(jnp.int32)

    for s in (-2, 2, -1, 1, 0):
        greet(on_one & (x >= 1), x - 1, collector(x - 1), s)
        onto = (on_one & (x >= 1) & (x <= 2)) | (jnp.logical_not(on_one) & (x == 0))
        greet(onto, x + 1, collector(x + 1), s)
    tail = jnp.where(x == 0, on_one, jnp.logical_not(on_one) & (x == 3))
    for s in (-1, 1, 0):
        to = jnp.where(x == 0, x + 1, x - 1)
        greet(tail, to, collector(to), s)

    for e in range(2):
        for s in (-2, -1, 1, 2):

            @pl.when(jnp.logical_not(exists(s)))
            def _():
                arrived[e, 2 + s] = jnp.zeros_like(arrived[e, 2 + s])

        for s in (-1, 1):

            @pl.when(jnp.logical_not(exists(s)))
            def _():
                at = e * SLOTS + 1 + s
                if e == 0:
                    first[1 + s] = jnp.zeros_like(first[1 + s])
                    beside[1 + s] = jnp.zeros_like(beside[1 + s])
                terms[at] = jnp.zeros_like(terms[at])
                bands[at] = jnp.zeros_like(bands[at])

    for copy in scalar_copies:
        copy.wait()
    slot_of = lax.broadcasted_iota(jnp.int32, (shots, shots), 0)
    shot_of = lax.broadcasted_iota(jnp.int32, (shots, shots), 1)
    wanted = jnp.zeros((shots, shots), jnp.int32)
    for j in range(shots):
        wanted = jnp.where(slot_of == j, order_ref[j], wanted)
    pick = (shot_of == wanted).astype(F32).astype(BF16)
    pltpu.make_async_copy(src, src, src_sem).wait()
    for d in range(2):
        term = jnp.dot(pick, src[d], preferred_element_type=F32).astype(BF16)
        terms[own_slot(d)] = term

        @pl.when(is_source(d))
        def _():
            result[d] = term
            if d == 1:
                first[HOME] = term

    place = []
    for t in range(count):
        row = rows_ref[t] - k * local
        col = cols_ref[t] - (k - 1) * local
        place.append(row * 3 * local + col)

    steps = TILE // PART
    early_slot = jnp.where(early == 0, own_slot(0), own_slot(1))
    late_slot = jnp.where(early == 0, own_slot(1), own_slot(0))

    def build(late, r):
        sweep = (early + late) % 2
        slot = late_slot if late else early_slot

        def step(part, carry):
            lines = pl.ds(pl.multiple_of(part * PART, PART), PART)
            pieces = [tiles[sweep, t, lines, :].astype(F32) for t in range(count)]
            for c in range(r, r + 5):
                total = jnp.zeros((PART, TILE), F32)
                for t in range(count):
                    total = total + jnp.where(place[t] == r * 3 * local + c, pieces[t], 0.0)
                at = pl.ds(pl.multiple_of(band_rows(c, r) + part * PART, PART), PART)
                bands[slot, at, :] = total.astype(BF16)
            return carry

        lax.fori_loop(0, steps, step, 0)

    def send(source, target, send_sem, recv_sem, x_to, core_to, s):
        return pltpu.make_async_remote_copy(
            src_ref=source,
            dst_ref=target,
            send_sem=send_sem,
            recv_sem=recv_sem,
            device_id=(x_to * 2 + core_to, k + s),
            device_id_type=MESH,
        )

    def await_recv(buffer, sem):
        pltpu.make_async_remote_copy(
            src_ref=buffer,
            dst_ref=buffer,
            send_sem=hand_send,
            recv_sem=sem,
            device_id=(layer, k),
            device_id_type=MESH,
        ).wait_recv()

    turn = 1 - 2 * (k % PLANE >= PLANE // 2).astype(jnp.int32)

    def leaves_plane(s):
        return (k % PLANE + s) // PLANE != 0

    def give(condition, d, seconds, lines=(0, 1)):
        for s in (0,) if seconds else (-1, 1, 0):
            remote = exists(s) if s else core != stage_core(d, x)
            kind = layer_in(d) == (1 if seconds else 0)

            @pl.when(condition & remote & kind & jnp.logical_not(is_source(d)))
            def _():
                at = own_slot(d)
                to = event_of(d) * SLOTS + (SECOND if seconds else 1 - s)

                def part(source, target, r):
                    return send(
                        source,
                        target,
                        band_send.at[2 if seconds else r],
                        band_recv.at[to],
                        x,
                        stage_core(d, x),
                        s,
                    )

                for r in lines:
                    piece = pl.ds(r * REACH, REACH)
                    part(bands.at[at, piece], bands.at[to, piece], r).start()
                    if r == 1:
                        part(terms.at[at], terms.at[to], r).start()

    def await_sent(condition, buffer, sem):
        @pl.when(condition)
        def _():
            send(buffer, buffer, sem, band_recv.at[0], x, partner, 0).wait_send()

    def await_given(condition, d, lines):
        targets = present(-1) + present(1) + (core != stage_core(d, x)).astype(jnp.int32)
        ours = condition & (layer_in(d) == 0) & jnp.logical_not(is_source(d))
        for n in (1, 2, 3):
            for r in lines:
                size = bands.at[pl.ds(0, n), pl.ds(0, REACH + r * TERM)]
                await_sent(ours & (targets == n), size, band_send.at[r])

    whole = bands.at[pl.ds(0, 2), pl.ds(0, REACH + TERM // 2)]

    def await_seconds(d):
        remote = core != stage_core(d, x)
        await_sent(remote & (layer_in(d) == 1), whole, band_send.at[2])

    def blocks(n):
        return arrived.at[0, pl.ds(0, n)]

    def sources(d):
        for s in (-1, 1, 0):
            remote = exists(s) if s else core != stage_core(d, x)

            @pl.when(is_source(d) & remote)
            def _():
                send(
                    terms.at[OUTGOING + d],
                    first.at[1 - s],
                    side_send,
                    trace_recv.at[0, 2 - s],
                    x,
                    stage_core(d, x),
                    s,
                ).start()

    def await_sources(d):
        targets = present(-1) + present(1) + (core != stage_core(d, x)).astype(jnp.int32)
        for n in (1, 2, 3):
            await_sent(is_source(d) & (targets == n), blocks(n), side_send)

    def await_forward(e):
        for n in (3, 4, 5):
            await_sent(spread == n, blocks(n), trace_send.at[e])
        if e == 1:
            for n in (2, 3):
                await_sent(reach == n, blocks(n), side_send)

    def forward(e):
        d = (early + e) % 2
        to = x + 1 - 2 * d
        slot = (stage_of(d) + 1) // 2

        def main(s):
            return send(
                second.at[e],
                arrived.at[slot, 2 - s],
                trace_send.at[e],
                trace_recv.at[slot, 2 - s],
                to,
                stage_core(d, to),
                s,
            )

        def extra(s):
            return send(
                second.at[e],
                beside.at[1 - s],
                side_send,
                trace_recv.at[1, 2 - s],
                to,
                1 - stage_core(d, to),
                s,
            )

        for crossing in (True, False):
            for copies, reached in ((main, (-1, 1)), (extra, (-1, 1)), (main, (-2, 2, 0)), (extra, (0,))):
                if copies is extra and e == 0:
                    continue
                for s in reached:
                    if crossing and s == 0:
                        continue
                    side = leaves_plane(s)

                    @pl.when(exists(s) & (side if crossing else jnp.logical_not(side)))
                    def _():
                        copies(s).start()

    def hand(e, d, from_second):
        return send(
            second.at[e] if from_second else centre.at[e],
            result.at[d],
            hand_send,
            hand_recv.at[d],
            x,
            partner,
            0,
        )

    origin = is_source(0) | is_source(1)

    pltpu.make_async_copy(tiles, tiles, tile_sem).wait()

    @pl.when(jnp.logical_not(origin))
    def _():
        build(0, 0)

    patient = jnp.logical_not(on_one) & (x >= 2)

    @pl.when(patient)
    def _():
        build(0, 1)

    reach = present(-1) + present(0) + present(1)
    spread = reach + present(-2) + present(2)
    onward = (x <= 2).astype(jnp.int32) + (x >= 1).astype(jnp.int32)
    between = (x >= 1) & (x <= 2)
    collects = core == collector(x)
    pl.semaphore_wait(
        barrier,
        reach
        + collects.astype(jnp.int32) * (onward * spread + between.astype(jnp.int32) * reach),
    )

    @pl.when(collects & (x >= 2))
    def _():
        pl.semaphore_signal(go, inc=1, device_id=(x * 2 + partner, k), device_id_type=MESH)

    for d in range(2):
        sources(d)
    for d in range(2):
        for seconds in (False, True):
            give(event_of(d) == 0, d, seconds, (0,))

    @pl.when(jnp.logical_not(origin | patient))
    def _():
        build(0, 1)

    for d in range(2):
        for seconds in (False, True):
            give(event_of(d) == 0, d, seconds, (1,))
    for r in range(2):
        build(1, r)
    for d in range(2):
        give(event_of(d) == 1, d, True)

    def let_go():
        pl.semaphore_signal(go, inc=1, device_id=(x * 2 + partner, k), device_id_type=MESH)

    leads = between & (core == early)
    follows = between & (core != early)
    for d in range(2):
        await_given(leads & (event_of(d) == 0), d, (0,))

    @pl.when(leads)
    def _():
        let_go()

    @pl.when(follows)
    def _():
        pl.semaphore_wait(go, 1)
        pl.delay(1300)

    for d in range(2):
        give(follows & (event_of(d) == 1), d, False)

    def event(e):
        d = (early + e) % 2
        X = stage_of(d)
        base = e * SLOTS
        ends_second = (d == 0) | (x == 0)

        def await_band(slot):
            here = exists(slot - 1)
            if slot is HOME:
                here = ends_second
            if slot is SECOND:
                here = jnp.logical_not(ends_second)

            @pl.when(here)
            def _():
                await_recv(whole, band_recv.at[base + slot])

        if e == 0:

            @pl.when(X == 0)
            def _():
                await_band(SECOND)
                total = terms[base + SECOND].astype(F32)
                for b in range(3):
                    outer[b] = band_block(bands, base + SECOND, b)
                for b in (HOME, 1 + turn, 1 - turn):

                    @pl.when(d == 0 if b is HOME else (k + b - 1 >= 0) & (k + b - 1 < devices))
                    def _():
                        await_recv(first.at[b], trace_recv.at[0, 1 + b])

                    total = total + times_all(first[b], outer[b])
                second[e] = total.astype(BF16)

        def await_block(block):
            @pl.when((k + block - 2 >= 0) & (k + block - 2 < devices))
            def _():
                await_recv(arrived.at[e, block], trace_recv.at[e, block])

        @pl.when(X >= 1)
        def _():
            await_band(SECOND)
            for t in range(3):
                outer[t] = band_block(bands, base + SECOND, t)
            for block in (0, 4):
                sums[block] = jnp.zeros_like(sums[block])
            total = terms[base + SECOND].astype(F32)
            for t in (HOME, 1 + turn, 1 - turn):
                await_band(t)
                total = total + times_all(terms[base + t], outer[t])
                for b in range(3):
                    product = jnp.dot(
                        outer[t], band_block(bands, base + t, b), preferred_element_type=F32
                    )
                    sums[t + b] = product if t is HOME else sums[t + b] + product
            for block in range(5):
                products[block] = sums[block].astype(BF16)
            for j in (0, 1, 2, -1, -2):
                block = 2 + j * turn
                await_block(block)
                total = total + times_all(arrived[e, block], products[block])
            second[e] = total.astype(BF16)

        if e == 0:

            @pl.when(x >= 2)
            def _():
                pl.semaphore_wait(go, 1)

        @pl.when(X < 3)
        def _():
            forward(e)

        @pl.when((X == 1) | (X == 2))
        def _():
            inner = terms[base + HOME].astype(F32)
            for b in range(3):
                inner = inner + times(arrived[e, 1 + b], bands, base + HOME, b)
            centre[e] = inner.astype(BF16)

            @pl.when(ends_second)
            def _():
                hand(e, d, False).start()

        @pl.when(ends_second)
        def _():
            result[d] = second[e]

        @pl.when(jnp.logical_not(ends_second))
        def _():
            hand(e, d, True).start()

            @pl.when(X >= 1)
            def _():
                result[d] = centre[e]

    @pl.when(on_one)
    def _():
        event(0)

    @pl.when(on_one & (x == 3))
    def _():
        let_go()

    @pl.when(jnp.logical_not(on_one) & (x == 3))
    def _():
        pl.semaphore_wait(go, 1)

    for d in range(2):
        give(((x == 0) | (x == 3)) & (event_of(d) == 1), d, False)

    late = on_one != (x == 0)

    def finish():
        for d in range(2):
            await_sources(d)
            led = leads & (event_of(d) == 0)
            await_given(led, d, (1,))
            await_given(jnp.logical_not(led), d, (0, 1))
            await_seconds(d)

        @pl.when(on_one)
        def _():
            await_forward(0)

        await_sent(on_one & (x == 3), blocks(1), hand_send)

    @pl.when(jnp.logical_not(between))
    def _():
        finish()

    @pl.when(late)
    def _():
        event(1)

    for d in range(2):
        last = stage_of(d) == 3

        @pl.when(tail & last)
        def _():
            at = OUTGOING + d
            total = terms[at].astype(F32)
            for b in range(3):
                outer[b] = band_block(bands, at, b)
            for b in (HOME, 1 + turn, 1 - turn):

                @pl.when((k + b - 1 >= 0) & (k + b - 1 < devices))
                def _():
                    await_recv(beside.at[b], trace_recv.at[1, 1 + b])

                total = total + times_all(beside[b], outer[b])
            result[d] = total.astype(BF16)

        @pl.when(jnp.logical_not(computes(d) | is_source(d) | last))
        def _():
            await_recv(result.at[d], hand_recv.at[d])

    out_ref[0] = (result[0].astype(F32) + result[1].astype(F32)).astype(BF16)

    @pl.when(between)
    def _():
        finish()

        @pl.when(late)
        def _():
            await_forward(1)
            await_sent(True, blocks(2), hand_send)


def shards(down_sources, up_sources, down_tiles, up_tiles, tile_rows, tile_cols, shot_order):
    shots, width = down_sources.shape[1:]
    count = down_tiles.shape[1]
    anywhere = pl.BlockSpec(memory_space=pl.ANY)
    dma = pltpu.SemaphoreType.DMA
    return pl.pallas_call(
        kernel,
        name="sweeps",
        out_shape=pltpu.VMEM(down_sources.shape, BF16),
        in_specs=[anywhere] * 7,
        out_specs=pl.BlockSpec(memory_space=pltpu.VMEM),
        scratch_shapes=[
            pltpu.SMEM((count,), jnp.int32),
            pltpu.SMEM((count,), jnp.int32),
            pltpu.SMEM(shot_order.shape, jnp.int32),
            pltpu.VMEM((2, shots, width), BF16),
            pltpu.VMEM((2, count, TILE, TILE), BF16),
            pltpu.VMEM((OUTGOING + 2, 10 * TILE, TILE), BF16),
            pltpu.VMEM((OUTGOING + 2, shots, width), BF16),
            pltpu.VMEM((3, shots, width), BF16),
            pltpu.VMEM((2, shots, width), BF16),
            pltpu.VMEM((2, shots, width), BF16),
            pltpu.VMEM((2, 5, shots, width), BF16),
            pltpu.VMEM((3, shots, width), BF16),
            pltpu.VMEM((3, width, width), BF16),
            pltpu.VMEM((5, width, width), F32),
            pltpu.VMEM((5, width, width), BF16),
            pltpu.VMEM((2, shots, width), BF16),
            dma((3,)),
            dma,
            dma,
            dma((3,)),
            dma((OUTGOING,)),
            dma,
            dma((2,)),
            dma((2, 5)),
            dma,
            dma((2,)),
            pltpu.SemaphoreType.REGULAR,
        ],
        compiler_params=pltpu.CompilerParams(collective_id=0, has_side_effects=True),
    )(tile_rows[0], tile_cols[0], shot_order, down_sources, up_sources, down_tiles, up_tiles)


def solution(mesh):
    return jax.shard_map(
        shards,
        mesh=mesh,
        in_specs=(
            P("layer", None, "rows"),
            P("layer", None, "rows"),
            P("layer", "rows", None, None),
            P("layer", "rows", None, None),
            P("layer", "rows"),
            P("layer", "rows"),
            P(),
        ),
        out_specs=P("layer", None, "rows"),
        check_vma=False,
    )
```

```python
import jax
import jax.numpy as jnp
from jax import lax
from jax.experimental import pallas as pl
from jax.experimental.pallas import tpu as pltpu
from jax.sharding import PartitionSpec as P

TILE = 128
MESH = pl.DeviceIdType.MESH
F32 = jnp.float32
BF16 = jnp.bfloat16
LEFT, HOME, RIGHT, SECOND = range(4)
SLOTS = 4
OUTGOING = 2 * SLOTS
PART = 16
PLANE = 4


REACH = 5 * TILE
TERM = 64


def band_rows(c, r):
    return r * REACH + (c - r) * TILE


def band_block(bands, slot, b):
    def tile(c, r):
        return bands[slot, pl.ds(band_rows(c, r), TILE), :]

    def line(r):
        pieces = [
            tile(c, r) if abs(c - 2 - r) <= 2 else jnp.zeros((TILE, TILE), BF16)
            for c in (2 * b, 2 * b + 1)
        ]
        return jnp.concatenate(pieces, axis=1)

    return jnp.concatenate([line(0), line(1)], axis=0)


def times_all(block, matrix):
    return lax.dot_general(
        block, matrix, (((1,), (1,)), ((), ())), preferred_element_type=F32
    )


def times(block, bands, slot, b):
    return times_all(block, band_block(bands, slot, b))


def kernel(
    rows_hbm,
    cols_hbm,
    order_hbm,
    down_src,
    up_src,
    down_tiles,
    up_tiles,
    out_ref,
    rows_ref,
    cols_ref,
    order_ref,
    src,
    tiles,
    bands,
    terms,
    first,
    centre,
    second,
    arrived,
    beside,
    outer,
    sums,
    products,
    result,
    scalar_sem,
    src_sem,
    tile_sem,
    band_send,
    band_recv,
    side_send,
    trace_send,
    trace_recv,
    hand_send,
    hand_recv,
    go,
):
    devices = lax.axis_size("rows")
    layer, k = lax.axis_index("layer"), lax.axis_index("rows")
    shots, width = src.shape[1], src.shape[2]
    local = width // TILE
    count = tiles.shape[1]
    x, core = layer // 2, layer % 2
    partner = 1 - core
    early = x // 2

    def stage_of(d):
        return x + d * (3 - 2 * x)

    def layer_in(d):
        return core + d * (1 - 2 * core)

    def stage_core(d, at):
        return 1 - d * (at == 0).astype(jnp.int32)

    def event_of(d):
        return stage_of(d) // 2

    def is_source(d):
        return (stage_of(d) == 0) & (layer_in(d) == 0)

    def computes(d):
        return core == stage_core(d, x)

    def own_slot(d):
        inside = event_of(d) * SLOTS + jnp.where(layer_in(d) == 0, HOME, SECOND)
        return jnp.where(computes(d) & jnp.logical_not(is_source(d)), inside, OUTGOING + d)

    scalar_copies = [
        pltpu.make_async_copy(a, b, scalar_sem.at[i])
        for i, (a, b) in enumerate(
            ((rows_hbm, rows_ref), (cols_hbm, cols_ref), (order_hbm, order_ref))
        )
    ]
    src_copies = [
        pltpu.make_async_copy(ref.at[0], src.at[d], src_sem)
        for d, ref in enumerate((down_src, up_src))
    ]
    tile_copies = [
        pltpu.make_async_copy(ref.at[0], tiles.at[d], tile_sem)
        for d, ref in enumerate((down_tiles, up_tiles))
    ]

    def exists(s):
        return (k + s >= 0) & (k + s < devices)

    def present(s):
        return exists(s).astype(jnp.int32)

    barrier = pltpu.get_barrier_semaphore()

    def greet(condition, x_to, core_to, s):
        @pl.when(condition & exists(s))
        def _():
            pl.semaphore_signal(
                barrier, inc=1, device_id=(x_to * 2 + core_to, k + s), device_id_type=MESH
            )

    on_one = core == 1
    for s in (-1, 1):
        greet(on_one | (x == 0), x, partner, s)
        greet(on_one & (x >= 1), x, core, s)
    greet(True, x, partner, 0)
    for copy in scalar_copies + src_copies + tile_copies:
        copy.start()
    def collector(x_to):
        return (x_to <= 1).astype(jnp.int32)

    for s in (-2, 2, -1, 1, 0):
        greet(on_one & (x >= 1), x - 1, collector(x - 1), s)
        onto = (on_one & (x >= 1) & (x <= 2)) | (jnp.logical_not(on_one) & (x == 0))
        greet(onto, x + 1, collector(x + 1), s)
    tail = jnp.where(x == 0, on_one, jnp.logical_not(on_one) & (x == 3))
    for s in (-1, 1, 0):
        to = jnp.where(x == 0, x + 1, x - 1)
        greet(tail, to, collector(to), s)

    for e in range(2):
        for s in (-2, -1, 1, 2):

            @pl.when(jnp.logical_not(exists(s)))
            def _():
                arrived[e, 2 + s] = jnp.zeros_like(arrived[e, 2 + s])

        for s in (-1, 1):

            @pl.when(jnp.logical_not(exists(s)))
            def _():
                at = e * SLOTS + 1 + s
                if e == 0:
                    first[1 + s] = jnp.zeros_like(first[1 + s])
                    beside[1 + s] = jnp.zeros_like(beside[1 + s])
                terms[at] = jnp.zeros_like(terms[at])
                bands[at] = jnp.zeros_like(bands[at])

    for copy in scalar_copies:
        copy.wait()
    slot_of = lax.broadcasted_iota(jnp.int32, (shots, shots), 0)
    shot_of = lax.broadcasted_iota(jnp.int32, (shots, shots), 1)
    wanted = jnp.zeros((shots, shots), jnp.int32)
    for j in range(shots):
        wanted = jnp.where(slot_of == j, order_ref[j], wanted)
    pick = (shot_of == wanted).astype(F32).astype(BF16)
    pltpu.make_async_copy(src, src, src_sem).wait()
    for d in range(2):
        term = jnp.dot(pick, src[d], preferred_element_type=F32).astype(BF16)
        terms[own_slot(d)] = term

        @pl.when(is_source(d))
        def _():
            result[d] = term
            if d == 1:
                first[HOME] = term

    place = []
    for t in range(count):
        row = rows_ref[t] - k * local
        col = cols_ref[t] - (k - 1) * local
        place.append(row * 3 * local + col)

    steps = TILE // PART
    early_slot = jnp.where(early == 0, own_slot(0), own_slot(1))
    late_slot = jnp.where(early == 0, own_slot(1), own_slot(0))

    def build(late, r):
        sweep = (early + late) % 2
        slot = late_slot if late else early_slot

        def step(part, carry):
            lines = pl.ds(pl.multiple_of(part * PART, PART), PART)
            pieces = [tiles[sweep, t, lines, :].astype(F32) for t in range(count)]
            for c in range(r, r + 5):
                total = jnp.zeros((PART, TILE), F32)
                for t in range(count):
                    total = total + jnp.where(place[t] == r * 3 * local + c, pieces[t], 0.0)
                at = pl.ds(pl.multiple_of(band_rows(c, r) + part * PART, PART), PART)
                bands[slot, at, :] = total.astype(BF16)
            return carry

        lax.fori_loop(0, steps, step, 0)

    def send(source, target, send_sem, recv_sem, x_to, core_to, s):
        return pltpu.make_async_remote_copy(
            src_ref=source,
            dst_ref=target,
            send_sem=send_sem,
            recv_sem=recv_sem,
            device_id=(x_to * 2 + core_to, k + s),
            device_id_type=MESH,
        )

    def await_recv(buffer, sem):
        pltpu.make_async_remote_copy(
            src_ref=buffer,
            dst_ref=buffer,
            send_sem=hand_send,
            recv_sem=sem,
            device_id=(layer, k),
            device_id_type=MESH,
        ).wait_recv()

    turn = 1 - 2 * (k % PLANE >= PLANE // 2).astype(jnp.int32)

    def leaves_plane(s):
        return (k % PLANE + s) // PLANE != 0

    def give(condition, d, seconds, lines=(0, 1)):
        for s in (0,) if seconds else (-1, 1, 0):
            remote = exists(s) if s else core != stage_core(d, x)
            kind = layer_in(d) == (1 if seconds else 0)

            @pl.when(condition & remote & kind & jnp.logical_not(is_source(d)))
            def _():
                at = own_slot(d)
                to = event_of(d) * SLOTS + (SECOND if seconds else 1 - s)

                def part(source, target, r):
                    return send(
                        source,
                        target,
                        band_send.at[2 if seconds else r],
                        band_recv.at[to],
                        x,
                        stage_core(d, x),
                        s,
                    )

                for r in lines:
                    piece = pl.ds(r * REACH, REACH)
                    part(bands.at[at, piece], bands.at[to, piece], r).start()
                    if r == 1:
                        part(terms.at[at], terms.at[to], r).start()

    def await_sent(condition, buffer, sem):
        @pl.when(condition)
        def _():
            send(buffer, buffer, sem, band_recv.at[0], x, partner, 0).wait_send()

    def await_given(condition, d, lines):
        targets = present(-1) + present(1) + (core != stage_core(d, x)).astype(jnp.int32)
        ours = condition & (layer_in(d) == 0) & jnp.logical_not(is_source(d))
        for n in (1, 2, 3):
            for r in lines:
                size = bands.at[pl.ds(0, n), pl.ds(0, REACH + r * TERM)]
                await_sent(ours & (targets == n), size, band_send.at[r])

    whole = bands.at[pl.ds(0, 2), pl.ds(0, REACH + TERM // 2)]

    def await_seconds(d):
        remote = core != stage_core(d, x)
        await_sent(remote & (layer_in(d) == 1), whole, band_send.at[2])

    def blocks(n):
        return arrived.at[0, pl.ds(0, n)]

    def sources(d):
        for s in (-1, 1, 0):
            remote = exists(s) if s else core != stage_core(d, x)

            @pl.when(is_source(d) & remote)
            def _():
                send(
                    terms.at[OUTGOING + d],
                    first.at[1 - s],
                    side_send,
                    trace_recv.at[0, 2 - s],
                    x,
                    stage_core(d, x),
                    s,
                ).start()

    def await_sources(d):
        targets = present(-1) + present(1) + (core != stage_core(d, x)).astype(jnp.int32)
        for n in (1, 2, 3):
            await_sent(is_source(d) & (targets == n), blocks(n), side_send)

    def await_forward(e):
        for n in (3, 4, 5):
            await_sent(spread == n, blocks(n), trace_send.at[e])
        if e == 1:
            for n in (2, 3):
                await_sent(reach == n, blocks(n), side_send)

    def forward(e):
        d = (early + e) % 2
        to = x + 1 - 2 * d
        slot = (stage_of(d) + 1) // 2

        def main(s):
            return send(
                second.at[e],
                arrived.at[slot, 2 - s],
                trace_send.at[e],
                trace_recv.at[slot, 2 - s],
                to,
                stage_core(d, to),
                s,
            )

        def extra(s):
            return send(
                second.at[e],
                beside.at[1 - s],
                side_send,
                trace_recv.at[1, 2 - s],
                to,
                1 - stage_core(d, to),
                s,
            )

        for crossing in (True, False):
            for copies, reached in ((main, (-1, 1)), (extra, (-1, 1)), (main, (-2, 2, 0)), (extra, (0,))):
                if copies is extra and e == 0:
                    continue
                for s in reached:
                    if crossing and s == 0:
                        continue
                    side = leaves_plane(s)

                    @pl.when(exists(s) & (side if crossing else jnp.logical_not(side)))
                    def _():
                        copies(s).start()

    def hand(e, d, from_second):
        return send(
            second.at[e] if from_second else centre.at[e],
            result.at[d],
            hand_send,
            hand_recv.at[d],
            x,
            partner,
            0,
        )

    origin = is_source(0) | is_source(1)

    pltpu.make_async_copy(tiles, tiles, tile_sem).wait()

    @pl.when(jnp.logical_not(origin))
    def _():
        build(0, 0)

    patient = jnp.logical_not(on_one) & (x >= 2)

    @pl.when(patient)
    def _():
        build(0, 1)

    reach = present(-1) + present(0) + present(1)
    spread = reach + present(-2) + present(2)
    onward = (x <= 2).astype(jnp.int32) + (x >= 1).astype(jnp.int32)
    between = (x >= 1) & (x <= 2)
    collects = core == collector(x)
    pl.semaphore_wait(
        barrier,
        reach
        + collects.astype(jnp.int32) * (onward * spread + between.astype(jnp.int32) * reach),
    )

    @pl.when(collects & (x >= 2))
    def _():
        pl.semaphore_signal(go, inc=1, device_id=(x * 2 + partner, k), device_id_type=MESH)

    for d in range(2):
        sources(d)
    for d in range(2):
        for seconds in (False, True):
            give(event_of(d) == 0, d, seconds, (0,))

    @pl.when(jnp.logical_not(origin | patient))
    def _():
        build(0, 1)

    for d in range(2):
        for seconds in (False, True):
            give(event_of(d) == 0, d, seconds, (1,))
    for r in range(2):
        build(1, r)
    for d in range(2):
        give(event_of(d) == 1, d, True)

    def let_go():
        pl.semaphore_signal(go, inc=1, device_id=(x * 2 + partner, k), device_id_type=MESH)

    leads = between & (core == early)
    follows = between & (core != early)
    for d in range(2):
        await_given(leads & (event_of(d) == 0), d, (0,))

    @pl.when(leads)
    def _():
        let_go()

    @pl.when(follows)
    def _():
        pl.semaphore_wait(go, 1)
        @pl.when(x == 1)
        def _():
            pl.delay(1000)

        @pl.when(x == 2)
        def _():
            pl.delay(1700)

    for d in range(2):
        give(follows & (event_of(d) == 1), d, False)

    def event(e):
        d = (early + e) % 2
        X = stage_of(d)
        base = e * SLOTS
        ends_second = (d == 0) | (x == 0)

        def await_band(slot):
            here = exists(slot - 1)
            if slot is HOME:
                here = ends_second
            if slot is SECOND:
                here = jnp.logical_not(ends_second)

            @pl.when(here)
            def _():
                await_recv(whole, band_recv.at[base + slot])

        if e == 0:

            @pl.when(X == 0)
            def _():
                await_band(SECOND)
                total = terms[base + SECOND].astype(F32)
                for b in range(3):
                    outer[b] = band_block(bands, base + SECOND, b)
                for b in (HOME, 1 + turn, 1 - turn):

                    @pl.when(d == 0 if b is HOME else (k + b - 1 >= 0) & (k + b - 1 < devices))
                    def _():
                        await_recv(first.at[b], trace_recv.at[0, 1 + b])

                    total = total + times_all(first[b], outer[b])
                second[e] = total.astype(BF16)

        def await_block(block):
            @pl.when((k + block - 2 >= 0) & (k + block - 2 < devices))
            def _():
                await_recv(arrived.at[e, block], trace_recv.at[e, block])

        @pl.when(X >= 1)
        def _():
            await_band(SECOND)
            for t in range(3):
                outer[t] = band_block(bands, base + SECOND, t)
            for block in (0, 4):
                sums[block] = jnp.zeros_like(sums[block])
            total = terms[base + SECOND].astype(F32)
            for t in (HOME, 1 + turn, 1 - turn):
                await_band(t)
                total = total + times_all(terms[base + t], outer[t])
                for b in range(3):
                    product = jnp.dot(
                        outer[t], band_block(bands, base + t, b), preferred_element_type=F32
                    )
                    sums[t + b] = product if t is HOME else sums[t + b] + product
            for block in range(5):
                products[block] = sums[block].astype(BF16)
            for j in (0, 1, 2, -1, -2):
                block = 2 + j * turn
                await_block(block)
                total = total + times_all(arrived[e, block], products[block])
            second[e] = total.astype(BF16)

        if e == 0:

            @pl.when(x >= 2)
            def _():
                pl.semaphore_wait(go, 1)

        @pl.when(X < 3)
        def _():
            forward(e)

        @pl.when((X == 1) | (X == 2))
        def _():
            inner = terms[base + HOME].astype(F32)
            for b in range(3):
                inner = inner + times(arrived[e, 1 + b], bands, base + HOME, b)
            centre[e] = inner.astype(BF16)

            @pl.when(ends_second)
            def _():
                hand(e, d, False).start()

        @pl.when(ends_second)
        def _():
            result[d] = second[e]

        @pl.when(jnp.logical_not(ends_second))
        def _():
            hand(e, d, True).start()

            @pl.when(X >= 1)
            def _():
                result[d] = centre[e]

    @pl.when(on_one)
    def _():
        event(0)

    @pl.when(on_one & (x == 3))
    def _():
        let_go()

    @pl.when(jnp.logical_not(on_one) & (x == 3))
    def _():
        pl.semaphore_wait(go, 1)

    for d in range(2):
        give(((x == 0) | (x == 3)) & (event_of(d) == 1), d, False)

    late = on_one != (x == 0)

    def finish():
        for d in range(2):
            await_sources(d)
            led = leads & (event_of(d) == 0)
            await_given(led, d, (1,))
            await_given(jnp.logical_not(led), d, (0, 1))
            await_seconds(d)

        @pl.when(on_one)
        def _():
            await_forward(0)

        await_sent(on_one & (x == 3), blocks(1), hand_send)

    @pl.when(jnp.logical_not(between))
    def _():
        finish()

    @pl.when(late)
    def _():
        event(1)

    for d in range(2):
        last = stage_of(d) == 3

        @pl.when(tail & last)
        def _():
            at = OUTGOING + d
            total = terms[at].astype(F32)
            for b in range(3):
                outer[b] = band_block(bands, at, b)
            for b in (HOME, 1 + turn, 1 - turn):

                @pl.when((k + b - 1 >= 0) & (k + b - 1 < devices))
                def _():
                    await_recv(beside.at[b], trace_recv.at[1, 1 + b])

                total = total + times_all(beside[b], outer[b])
            result[d] = total.astype(BF16)

        @pl.when(jnp.logical_not(computes(d) | is_source(d) | last))
        def _():
            await_recv(result.at[d], hand_recv.at[d])

    out_ref[0] = (result[0].astype(F32) + result[1].astype(F32)).astype(BF16)

    @pl.when(between)
    def _():
        finish()

        @pl.when(late)
        def _():
            await_forward(1)
            await_sent(True, blocks(2), hand_send)


def shards(down_sources, up_sources, down_tiles, up_tiles, tile_rows, tile_cols, shot_order):
    shots, width = down_sources.shape[1:]
    count = down_tiles.shape[1]
    anywhere = pl.BlockSpec(memory_space=pl.ANY)
    dma = pltpu.SemaphoreType.DMA
    return pl.pallas_call(
        kernel,
        name="sweeps",
        out_shape=pltpu.VMEM(down_sources.shape, BF16),
        in_specs=[anywhere] * 7,
        out_specs=pl.BlockSpec(memory_space=pltpu.VMEM),
        scratch_shapes=[
            pltpu.SMEM((count,), jnp.int32),
            pltpu.SMEM((count,), jnp.int32),
            pltpu.SMEM(shot_order.shape, jnp.int32),
            pltpu.VMEM((2, shots, width), BF16),
            pltpu.VMEM((2, count, TILE, TILE), BF16),
            pltpu.VMEM((OUTGOING + 2, 10 * TILE, TILE), BF16),
            pltpu.VMEM((OUTGOING + 2, shots, width), BF16),
            pltpu.VMEM((3, shots, width), BF16),
            pltpu.VMEM((2, shots, width), BF16),
            pltpu.VMEM((2, shots, width), BF16),
            pltpu.VMEM((2, 5, shots, width), BF16),
            pltpu.VMEM((3, shots, width), BF16),
            pltpu.VMEM((3, width, width), BF16),
            pltpu.VMEM((5, width, width), F32),
            pltpu.VMEM((5, width, width), BF16),
            pltpu.VMEM((2, shots, width), BF16),
            dma((3,)),
            dma,
            dma,
            dma((3,)),
            dma((OUTGOING,)),
            dma,
            dma((2,)),
            dma((2, 5)),
            dma,
            dma((2,)),
            pltpu.SemaphoreType.REGULAR,
        ],
        compiler_params=pltpu.CompilerParams(collective_id=0, has_side_effects=True),
    )(tile_rows[0], tile_cols[0], shot_order, down_sources, up_sources, down_tiles, up_tiles)


def solution(mesh):
    return jax.shard_map(
        shards,
        mesh=mesh,
        in_specs=(
            P("layer", None, "rows"),
            P("layer", None, "rows"),
            P("layer", "rows", None, None),
            P("layer", "rows", None, None),
            P("layer", "rows"),
            P("layer", "rows"),
            P(),
        ),
        out_specs=P("layer", None, "rows"),
        check_vma=False,
    )
```

```python
import jax
import jax.numpy as jnp
from jax import lax
from jax.experimental import pallas as pl
from jax.experimental.pallas import tpu as pltpu
from jax.sharding import PartitionSpec as P

TILE = 128
MESH = pl.DeviceIdType.MESH
F32 = jnp.float32
BF16 = jnp.bfloat16
LEFT, HOME, RIGHT, SECOND = range(4)
SLOTS = 4
OUTGOING = 2 * SLOTS
PART = 16
PLANE = 4


REACH = 5 * TILE
TERM = 64


def band_rows(c, r):
    return r * REACH + (c - r) * TILE


def band_block(bands, slot, b):
    def tile(c, r):
        return bands[slot, pl.ds(band_rows(c, r), TILE), :]

    def line(r):
        pieces = [
            tile(c, r) if abs(c - 2 - r) <= 2 else jnp.zeros((TILE, TILE), BF16)
            for c in (2 * b, 2 * b + 1)
        ]
        return jnp.concatenate(pieces, axis=1)

    return jnp.concatenate([line(0), line(1)], axis=0)


def times_all(block, matrix):
    return lax.dot_general(
        block, matrix, (((1,), (1,)), ((), ())), preferred_element_type=F32
    )


def times(block, bands, slot, b):
    return times_all(block, band_block(bands, slot, b))


def kernel(
    rows_hbm,
    cols_hbm,
    order_hbm,
    down_src,
    up_src,
    down_tiles,
    up_tiles,
    out_ref,
    rows_ref,
    cols_ref,
    order_ref,
    src,
    tiles,
    bands,
    terms,
    first,
    centre,
    second,
    arrived,
    beside,
    outer,
    sums,
    products,
    result,
    scalar_sem,
    src_sem,
    tile_sem,
    band_send,
    band_recv,
    side_send,
    trace_send,
    trace_recv,
    hand_send,
    hand_recv,
    go,
):
    devices = lax.axis_size("rows")
    layer, k = lax.axis_index("layer"), lax.axis_index("rows")
    shots, width = src.shape[1], src.shape[2]
    local = width // TILE
    count = tiles.shape[1]
    x, core = layer // 2, layer % 2
    partner = 1 - core
    early = x // 2

    def stage_of(d):
        return x + d * (3 - 2 * x)

    def layer_in(d):
        return core + d * (1 - 2 * core)

    def stage_core(d, at):
        return 1 - d * (at == 0).astype(jnp.int32)

    def event_of(d):
        return stage_of(d) // 2

    def is_source(d):
        return (stage_of(d) == 0) & (layer_in(d) == 0)

    def computes(d):
        return core == stage_core(d, x)

    def own_slot(d):
        inside = event_of(d) * SLOTS + jnp.where(layer_in(d) == 0, HOME, SECOND)
        return jnp.where(computes(d) & jnp.logical_not(is_source(d)), inside, OUTGOING + d)

    scalar_copies = [
        pltpu.make_async_copy(a, b, scalar_sem.at[i])
        for i, (a, b) in enumerate(
            ((rows_hbm, rows_ref), (cols_hbm, cols_ref), (order_hbm, order_ref))
        )
    ]
    src_copies = [
        pltpu.make_async_copy(ref.at[0], src.at[d], src_sem)
        for d, ref in enumerate((down_src, up_src))
    ]
    tile_copies = [
        pltpu.make_async_copy(ref.at[0], tiles.at[d], tile_sem)
        for d, ref in enumerate((down_tiles, up_tiles))
    ]

    def exists(s):
        return (k + s >= 0) & (k + s < devices)

    def present(s):
        return exists(s).astype(jnp.int32)

    barrier = pltpu.get_barrier_semaphore()

    def greet(condition, x_to, core_to, s):
        @pl.when(condition & exists(s))
        def _():
            pl.semaphore_signal(
                barrier, inc=1, device_id=(x_to * 2 + core_to, k + s), device_id_type=MESH
            )

    on_one = core == 1
    for s in (-1, 1):
        greet(on_one | (x == 0), x, partner, s)
        greet(on_one & (x >= 1), x, core, s)
    greet(True, x, partner, 0)
    for copy in scalar_copies + src_copies + tile_copies:
        copy.start()
    def collector(x_to):
        return (x_to <= 1).astype(jnp.int32)

    for s in (-2, 2, -1, 1, 0):
        greet(on_one & (x >= 1), x - 1, collector(x - 1), s)
        onto = (on_one & (x >= 1) & (x <= 2)) | (jnp.logical_not(on_one) & (x == 0))
        greet(onto, x + 1, collector(x + 1), s)
    tail = jnp.where(x == 0, on_one, jnp.logical_not(on_one) & (x == 3))
    for s in (-1, 1, 0):
        to = jnp.where(x == 0, x + 1, x - 1)
        greet(tail, to, collector(to), s)

    for e in range(2):
        for s in (-2, -1, 1, 2):

            @pl.when(jnp.logical_not(exists(s)))
            def _():
                arrived[e, 2 + s] = jnp.zeros_like(arrived[e, 2 + s])

        for s in (-1, 1):

            @pl.when(jnp.logical_not(exists(s)))
            def _():
                at = e * SLOTS + 1 + s
                if e == 0:
                    first[1 + s] = jnp.zeros_like(first[1 + s])
                    beside[1 + s] = jnp.zeros_like(beside[1 + s])
                terms[at] = jnp.zeros_like(terms[at])
                bands[at] = jnp.zeros_like(bands[at])

    for copy in scalar_copies:
        copy.wait()
    slot_of = lax.broadcasted_iota(jnp.int32, (shots, shots), 0)
    shot_of = lax.broadcasted_iota(jnp.int32, (shots, shots), 1)
    wanted = jnp.zeros((shots, shots), jnp.int32)
    for j in range(shots):
        wanted = jnp.where(slot_of == j, order_ref[j], wanted)
    pick = (shot_of == wanted).astype(F32).astype(BF16)
    pltpu.make_async_copy(src, src, src_sem).wait()
    for d in range(2):
        term = jnp.dot(pick, src[d], preferred_element_type=F32).astype(BF16)
        terms[own_slot(d)] = term

        @pl.when(is_source(d))
        def _():
            result[d] = term
            if d == 1:
                first[HOME] = term

    place = []
    for t in range(count):
        row = rows_ref[t] - k * local
        col = cols_ref[t] - (k - 1) * local
        place.append(row * 3 * local + col)

    steps = TILE // PART
    early_slot = jnp.where(early == 0, own_slot(0), own_slot(1))
    late_slot = jnp.where(early == 0, own_slot(1), own_slot(0))

    def build(late, r):
        sweep = (early + late) % 2
        slot = late_slot if late else early_slot

        def step(part, carry):
            lines = pl.ds(pl.multiple_of(part * PART, PART), PART)
            pieces = [tiles[sweep, t, lines, :].astype(F32) for t in range(count)]
            for c in range(r, r + 5):
                total = jnp.zeros((PART, TILE), F32)
                for t in range(count):
                    total = total + jnp.where(place[t] == r * 3 * local + c, pieces[t], 0.0)
                at = pl.ds(pl.multiple_of(band_rows(c, r) + part * PART, PART), PART)
                bands[slot, at, :] = total.astype(BF16)
            return carry

        lax.fori_loop(0, steps, step, 0)

    def send(source, target, send_sem, recv_sem, x_to, core_to, s):
        return pltpu.make_async_remote_copy(
            src_ref=source,
            dst_ref=target,
            send_sem=send_sem,
            recv_sem=recv_sem,
            device_id=(x_to * 2 + core_to, k + s),
            device_id_type=MESH,
        )

    def await_recv(buffer, sem):
        pltpu.make_async_remote_copy(
            src_ref=buffer,
            dst_ref=buffer,
            send_sem=hand_send,
            recv_sem=sem,
            device_id=(layer, k),
            device_id_type=MESH,
        ).wait_recv()

    turn = 1 - 2 * (k % PLANE >= PLANE // 2).astype(jnp.int32)

    def leaves_plane(s):
        return (k % PLANE + s) // PLANE != 0

    def give(condition, d, seconds, lines=(0, 1)):
        for s in (0,) if seconds else (-1, 1, 0):
            remote = exists(s) if s else core != stage_core(d, x)
            kind = layer_in(d) == (1 if seconds else 0)

            @pl.when(condition & remote & kind & jnp.logical_not(is_source(d)))
            def _():
                at = own_slot(d)
                to = event_of(d) * SLOTS + (SECOND if seconds else 1 - s)

                def part(source, target, r):
                    return send(
                        source,
                        target,
                        band_send.at[2 if seconds else r],
                        band_recv.at[to],
                        x,
                        stage_core(d, x),
                        s,
                    )

                for r in lines:
                    piece = pl.ds(r * REACH, REACH)
                    part(bands.at[at, piece], bands.at[to, piece], r).start()
                    if r == 1:
                        part(terms.at[at], terms.at[to], r).start()

    def await_sent(condition, buffer, sem):
        @pl.when(condition)
        def _():
            send(buffer, buffer, sem, band_recv.at[0], x, partner, 0).wait_send()

    def await_given(condition, d, lines):
        targets = present(-1) + present(1) + (core != stage_core(d, x)).astype(jnp.int32)
        ours = condition & (layer_in(d) == 0) & jnp.logical_not(is_source(d))
        for n in (1, 2, 3):
            for r in lines:
                size = bands.at[pl.ds(0, n), pl.ds(0, REACH + r * TERM)]
                await_sent(ours & (targets == n), size, band_send.at[r])

    whole = bands.at[pl.ds(0, 2), pl.ds(0, REACH + TERM // 2)]

    def await_seconds(d):
        remote = core != stage_core(d, x)
        await_sent(remote & (layer_in(d) == 1), whole, band_send.at[2])

    def blocks(n):
        return arrived.at[0, pl.ds(0, n)]

    def sources(d):
        for s in (-1, 1, 0):
            remote = exists(s) if s else core != stage_core(d, x)

            @pl.when(is_source(d) & remote)
            def _():
                send(
                    terms.at[OUTGOING + d],
                    first.at[1 - s],
                    side_send,
                    trace_recv.at[0, 2 - s],
                    x,
                    stage_core(d, x),
                    s,
                ).start()

    def await_sources(d):
        targets = present(-1) + present(1) + (core != stage_core(d, x)).astype(jnp.int32)
        for n in (1, 2, 3):
            await_sent(is_source(d) & (targets == n), blocks(n), side_send)

    def await_forward(e):
        for n in (3, 4, 5):
            await_sent(spread == n, blocks(n), trace_send.at[e])
        if e == 1:
            for n in (2, 3):
                await_sent(reach == n, blocks(n), side_send)

    def forward(e):
        d = (early + e) % 2
        to = x + 1 - 2 * d
        slot = (stage_of(d) + 1) // 2

        def main(s):
            return send(
                second.at[e],
                arrived.at[slot, 2 - s],
                trace_send.at[e],
                trace_recv.at[slot, 2 - s],
                to,
                stage_core(d, to),
                s,
            )

        def extra(s):
            return send(
                second.at[e],
                beside.at[1 - s],
                side_send,
                trace_recv.at[1, 2 - s],
                to,
                1 - stage_core(d, to),
                s,
            )

        for crossing in (True, False):
            for copies, reached in ((main, (-1, 1)), (extra, (-1, 1)), (main, (-2, 2, 0)), (extra, (0,))):
                if copies is extra and e == 0:
                    continue
                for s in reached:
                    if crossing and s == 0:
                        continue
                    side = leaves_plane(s)

                    @pl.when(exists(s) & (side if crossing else jnp.logical_not(side)))
                    def _():
                        copies(s).start()

    def hand(e, d, from_second):
        return send(
            second.at[e] if from_second else centre.at[e],
            result.at[d],
            hand_send,
            hand_recv.at[d],
            x,
            partner,
            0,
        )

    origin = is_source(0) | is_source(1)

    pltpu.make_async_copy(tiles, tiles, tile_sem).wait()

    @pl.when(jnp.logical_not(origin))
    def _():
        build(0, 0)

    patient = jnp.logical_not(on_one) & (x >= 2)

    @pl.when(patient)
    def _():
        build(0, 1)

    reach = present(-1) + present(0) + present(1)
    spread = reach + present(-2) + present(2)
    onward = (x <= 2).astype(jnp.int32) + (x >= 1).astype(jnp.int32)
    between = (x >= 1) & (x <= 2)
    collects = core == collector(x)
    pl.semaphore_wait(
        barrier,
        reach
        + collects.astype(jnp.int32) * (onward * spread + between.astype(jnp.int32) * reach),
    )

    @pl.when(collects & (x >= 2))
    def _():
        pl.semaphore_signal(go, inc=1, device_id=(x * 2 + partner, k), device_id_type=MESH)

    for d in range(2):
        sources(d)
    for d in range(2):
        for seconds in (False, True):
            give(event_of(d) == 0, d, seconds, (0,))

    @pl.when(jnp.logical_not(origin | patient))
    def _():
        build(0, 1)

    for d in range(2):
        for seconds in (False, True):
            give(event_of(d) == 0, d, seconds, (1,))
    for r in range(2):
        build(1, r)
    for d in range(2):
        give(event_of(d) == 1, d, True)

    def let_go():
        pl.semaphore_signal(go, inc=1, device_id=(x * 2 + partner, k), device_id_type=MESH)

    leads = between & (core == early)
    follows = between & (core != early)
    for d in range(2):
        await_given(leads & (event_of(d) == 0), d, (0,))

    @pl.when(leads)
    def _():
        let_go()

    @pl.when(follows)
    def _():
        pl.semaphore_wait(go, 1)
        pl.delay(1300)

    for d in range(2):
        give(follows & (event_of(d) == 1), d, False)

    def event(e):
        d = (early + e) % 2
        X = stage_of(d)
        base = e * SLOTS
        ends_second = (d == 0) | (x == 0)

        def await_band(slot):
            here = exists(slot - 1)
            if slot is HOME:
                here = ends_second
            if slot is SECOND:
                here = jnp.logical_not(ends_second)

            @pl.when(here)
            def _():
                await_recv(whole, band_recv.at[base + slot])

        if e == 0:

            @pl.when(X == 0)
            def _():
                await_band(SECOND)
                total = terms[base + SECOND].astype(F32)
                for b in range(3):
                    outer[b] = band_block(bands, base + SECOND, b)
                for b in (HOME, 1 + turn, 1 - turn):

                    @pl.when(d == 0 if b is HOME else (k + b - 1 >= 0) & (k + b - 1 < devices))
                    def _():
                        await_recv(first.at[b], trace_recv.at[0, 1 + b])

                    total = total + times_all(first[b], outer[b])
                second[e] = total.astype(BF16)

        def await_block(block):
            @pl.when((k + block - 2 >= 0) & (k + block - 2 < devices))
            def _():
                await_recv(arrived.at[e, block], trace_recv.at[e, block])

        @pl.when(X >= 1)
        def _():
            await_band(SECOND)
            for t in range(3):
                outer[t] = band_block(bands, base + SECOND, t)
            for block in (0, 4):
                sums[block] = jnp.zeros_like(sums[block])
            total = terms[base + SECOND].astype(F32)
            for t in (HOME, 1 + turn, 1 - turn):
                await_band(t)
                total = total + times_all(terms[base + t], outer[t])
                for b in range(3):
                    product = jnp.dot(
                        outer[t], band_block(bands, base + t, b), preferred_element_type=F32
                    )
                    sums[t + b] = product if t is HOME else sums[t + b] + product
            for block in range(5):
                products[block] = sums[block].astype(BF16)
            for j in (0, 1, 2, -1, -2):
                block = 2 + j * turn
                await_block(block)
                total = total + times_all(arrived[e, block], products[block])
            second[e] = total.astype(BF16)

        if e == 0:

            @pl.when(x >= 2)
            def _():
                pl.semaphore_wait(go, 1)

        @pl.when(X < 3)
        def _():
            forward(e)

        @pl.when((X == 1) | (X == 2))
        def _():
            inner = terms[base + HOME].astype(F32)
            for b in range(3):
                inner = inner + times(arrived[e, 1 + b], bands, base + HOME, b)
            centre[e] = inner.astype(BF16)

            @pl.when(ends_second)
            def _():
                hand(e, d, False).start()

        @pl.when(ends_second)
        def _():
            result[d] = second[e]

        @pl.when(jnp.logical_not(ends_second))
        def _():
            hand(e, d, True).start()

            @pl.when(X >= 1)
            def _():
                result[d] = centre[e]

    @pl.when(on_one)
    def _():
        event(0)

    @pl.when(on_one & (x == 3))
    def _():
        let_go()

    @pl.when(jnp.logical_not(on_one) & (x == 3))
    def _():
        pl.semaphore_wait(go, 1)

    @pl.when(((x == 0) & on_one) | ((x == 3) & jnp.logical_not(on_one)))
    def _():
        pl.delay(1500)

    for d in range(2):
        give(((x == 0) | (x == 3)) & (event_of(d) == 1), d, False)

    late = on_one != (x == 0)

    def finish():
        for d in range(2):
            await_sources(d)
            led = leads & (event_of(d) == 0)
            await_given(led, d, (1,))
            await_given(jnp.logical_not(led), d, (0, 1))
            await_seconds(d)

        @pl.when(on_one)
        def _():
            await_forward(0)

        await_sent(on_one & (x == 3), blocks(1), hand_send)

    @pl.when(jnp.logical_not(between))
    def _():
        finish()

    @pl.when(late)
    def _():
        event(1)

    for d in range(2):
        last = stage_of(d) == 3

        @pl.when(tail & last)
        def _():
            at = OUTGOING + d
            total = terms[at].astype(F32)
            for b in range(3):
                outer[b] = band_block(bands, at, b)
            for b in (HOME, 1 + turn, 1 - turn):

                @pl.when((k + b - 1 >= 0) & (k + b - 1 < devices))
                def _():
                    await_recv(beside.at[b], trace_recv.at[1, 1 + b])

                total = total + times_all(beside[b], outer[b])
            result[d] = total.astype(BF16)

        @pl.when(jnp.logical_not(computes(d) | is_source(d) | last))
        def _():
            await_recv(result.at[d], hand_recv.at[d])

    out_ref[0] = (result[0].astype(F32) + result[1].astype(F32)).astype(BF16)

    @pl.when(between)
    def _():
        finish()

        @pl.when(late)
        def _():
            await_forward(1)
            await_sent(True, blocks(2), hand_send)


def shards(down_sources, up_sources, down_tiles, up_tiles, tile_rows, tile_cols, shot_order):
    shots, width = down_sources.shape[1:]
    count = down_tiles.shape[1]
    anywhere = pl.BlockSpec(memory_space=pl.ANY)
    dma = pltpu.SemaphoreType.DMA
    return pl.pallas_call(
        kernel,
        name="sweeps",
        out_shape=pltpu.VMEM(down_sources.shape, BF16),
        in_specs=[anywhere] * 7,
        out_specs=pl.BlockSpec(memory_space=pltpu.VMEM),
        scratch_shapes=[
            pltpu.SMEM((count,), jnp.int32),
            pltpu.SMEM((count,), jnp.int32),
            pltpu.SMEM(shot_order.shape, jnp.int32),
            pltpu.VMEM((2, shots, width), BF16),
            pltpu.VMEM((2, count, TILE, TILE), BF16),
            pltpu.VMEM((OUTGOING + 2, 10 * TILE, TILE), BF16),
            pltpu.VMEM((OUTGOING + 2, shots, width), BF16),
            pltpu.VMEM((3, shots, width), BF16),
            pltpu.VMEM((2, shots, width), BF16),
            pltpu.VMEM((2, shots, width), BF16),
            pltpu.VMEM((2, 5, shots, width), BF16),
            pltpu.VMEM((3, shots, width), BF16),
            pltpu.VMEM((3, width, width), BF16),
            pltpu.VMEM((5, width, width), F32),
            pltpu.VMEM((5, width, width), BF16),
            pltpu.VMEM((2, shots, width), BF16),
            dma((3,)),
            dma,
            dma,
            dma((3,)),
            dma((OUTGOING,)),
            dma,
            dma((2,)),
            dma((2, 5)),
            dma,
            dma((2,)),
            pltpu.SemaphoreType.REGULAR,
        ],
        compiler_params=pltpu.CompilerParams(collective_id=0, has_side_effects=True),
    )(tile_rows[0], tile_cols[0], shot_order, down_sources, up_sources, down_tiles, up_tiles)


def solution(mesh):
    return jax.shard_map(
        shards,
        mesh=mesh,
        in_specs=(
            P("layer", None, "rows"),
            P("layer", None, "rows"),
            P("layer", "rows", None, None),
            P("layer", "rows", None, None),
            P("layer", "rows"),
            P("layer", "rows"),
            P(),
        ),
        out_specs=P("layer", None, "rows"),
        check_vma=False,
    )
```
